32 devices in a mesh: ctx: 16 (over z, y, core), tp: 2 (over x).
Axes of the slice: x: 2, y: 2, z: 4, core: 2. Of those that a mesh axis runs over, the one named last changes fastest.
Arguments:
- query: bfloat16 [2048, 4096], P('ctx', 'tp'), may hold values from -6 to 6
- key_in: bfloat16 [2048, 4096], P('ctx', 'tp'), may hold values from -6 to 6
- value: bfloat16 [2048, 4096], P('ctx', 'tp'), may hold values from -6 to 6
- short_taps: float32 [3, 3, 4096], P(None, None, 'tp'), may hold values from -3.5 to 3.5
- skip_gain: float32 [4096], P('tp'), may hold values from -1 to 1
- filter_spectrum: float32 [2048, 2, 2, 4096], P('ctx', None, None, 'tp'), may hold values from -6 to 6
- out_weight: bfloat16 [4096, 4096], P('tp'), may hold values from -0.09375 to 0.09375
Outputs:
- mixed_out: bfloat16 [2048, 4096], P('ctx', 'tp')
The draws below stay inside these ranges and needn't reach their ends.
All inputs are finite; a program needn't handle non-finite values.
Results may differ from the reference program's by a relative error of at most 0.0049.
Values may be sent and summed in bfloat16 or wider, within the bound.
No kernel may reach another device: no remote copies, remote signals or barrier semaphores. Data moves between devices by JAX's collectives and lax.ppermute only.
A program may use at most 128 MiB of HBM per device.

```python
import jax
import jax.numpy as jnp
from jax import lax

D = 4096
TAPS = 3
L = 2048


def steps_of(own_key, shape, shards, least, largest):
    level = 1.0
    for dim, parts in shards:
        steps = jax.random.uniform(jax.random.fold_in(jax.random.fold_in(own_key, 6), dim), (parts,), jnp.float32, least / len(shards), largest / len(shards))
        level = level * jnp.repeat(jnp.exp(steps), shape[dim] // parts).reshape((-1,) + (1,) * (len(shape) - 1 - dim))
    return level


def gaussian(stream_key, dims, spread, most, pieces=(), held_as=jnp.bfloat16):
    result = jax.random.normal(stream_key, dims, jnp.float32) * spread
    if len(pieces) > 0:
        result = steps_of(stream_key, dims, pieces, -0.22, 0.18) * result
    return jnp.clip(result, min=-most, max=most).astype(held_as)


def setup_inputs(seed: int = 0) -> dict:
    key_of = jax.random.split(jax.random.key(seed), 8)
    return {
        "query": gaussian(key_of[0], (L, D), 1.0, 6.0, ((0, 16), (1, 2))),
        "key_in": gaussian(key_of[1], (L, D), 1.0, 6.0, ((0, 16), (1, 2))),
        "value": gaussian(key_of[2], (L, D), 1.0, 6.0, ((0, 16), (1, 2))),
        "short_taps": gaussian(key_of[3], (3, TAPS, D), TAPS ** -0.5, 3.5, ((2, 2),), jnp.float32),
        "skip_gain": jnp.clip(jax.random.uniform(key_of[4], (D,), jnp.float32, -1.0, 1.0) * steps_of(key_of[4], (D,), ((0, 2),), -0.4, 0.0), -1.0, 1.0),
        "filter_spectrum": gaussian(key_of[5], (L, 2, 2, D), 1.0, 6.0, ((0, 16), (3, 2)), jnp.float32),
        "out_weight": gaussian(key_of[6], (D, D), D ** -0.5, 0.09375, ((0, 2),)),
    }


def causal_filter(signal, tap_weights):
    values = signal.astype(jnp.float32)
    padded = jnp.pad(values, ((2, 0), (0, 0)))
    return tap_weights[0] * values + tap_weights[1] * padded[1:-1] + tap_weights[2] * padded[:-2]


def reference(query, key_in, value, short_taps, skip_gain, filter_spectrum, out_weight):
    gate_signal = causal_filter(query, short_taps[0])
    mixed_in = causal_filter(key_in, short_taps[1]) * causal_filter(value, short_taps[2])
    length = mixed_in.shape[0]
    padded_length = 2 * length
    transformed = jnp.fft.fft(mixed_in, n=padded_length, axis=0)
    flat_spectrum = filter_spectrum.reshape(padded_length, 2, filter_spectrum.shape[3])
    product = transformed * lax.complex(flat_spectrum[:, 0], flat_spectrum[:, 1])
    convolved = jnp.real(jnp.fft.ifft(product, axis=0))[:length]
    mixed = convolved + skip_gain * mixed_in
    gated = (gate_signal * mixed).astype(jnp.bfloat16)
    return jnp.dot(gated, out_weight, preferred_element_type=jnp.float32).astype(jnp.bfloat16)
```

```python
import math

import jax
import jax.numpy as jnp
from jax import lax
from jax.sharding import PartitionSpec as P


def shifted_in(rows, axis):
    count = lax.axis_size(axis)
    return lax.ppermute(rows, axis, [(i, i + 1) for i in range(count - 1)])


def causal_filter(signal, tail, taps):
    values = jnp.concatenate([tail, signal], axis=0).astype(jnp.float32)
    return taps[0] * values[2:] + taps[1] * values[1:-1] + taps[2] * values[:-2]


def turn(rows, columns, order):
    index = rows[:, None] * columns[None, :] % order
    angle = (2.0 * math.pi / order) * index.astype(jnp.float32)
    return jnp.cos(angle), jnp.sin(angle)


def exact_dot(left, right):
    return jnp.dot(left, right, precision=lax.Precision.HIGHEST, preferred_element_type=jnp.float32)


def radix_of(order):
    return 2 ** ((order.bit_length() - 1) // 2)


def long_filter(signal, spectrum_real, spectrum_imag):
    length, width = signal.shape
    order = spectrum_real.shape[0]
    radix = radix_of(order)
    span, depth = order // radix, length // radix
    low = jnp.arange(span, dtype=jnp.int32)
    deep = jnp.arange(depth, dtype=jnp.int32)
    lanes = jnp.arange(radix, dtype=jnp.int32)
    inner_cos, inner_sin = turn(low, deep, span)
    twiddle_cos, twiddle_sin = (t[:, :, None] for t in turn(lanes, low, order))
    outer_cos, outer_sin = turn(lanes, lanes, radix)

    samples = signal.astype(jnp.float32).reshape(depth, radix * width)
    real = exact_dot(inner_cos, samples).reshape(span, radix, width).transpose(1, 0, 2)
    imag = -exact_dot(inner_sin, samples).reshape(span, radix, width).transpose(1, 0, 2)
    real, imag = (
        (real * twiddle_cos + imag * twiddle_sin).reshape(radix, span * width),
        (imag * twiddle_cos - real * twiddle_sin).reshape(radix, span * width),
    )
    real, imag = (
        exact_dot(outer_cos, real) + exact_dot(outer_sin, imag),
        exact_dot(outer_cos, imag) - exact_dot(outer_sin, real),
    )
    spectrum_real = spectrum_real.astype(jnp.float32).reshape(radix, span * width)
    spectrum_imag = spectrum_imag.astype(jnp.float32).reshape(radix, span * width)
    real, imag = (
        real * spectrum_real - imag * spectrum_imag,
        real * spectrum_imag + imag * spectrum_real,
    )
    real, imag = (
        (exact_dot(outer_cos, real) - exact_dot(outer_sin, imag)).reshape(radix, span, width),
        (exact_dot(outer_cos, imag) + exact_dot(outer_sin, real)).reshape(radix, span, width),
    )
    real, imag = (
        (real * twiddle_cos - imag * twiddle_sin).transpose(1, 0, 2).reshape(span, radix * width),
        (imag * twiddle_cos + real * twiddle_sin).transpose(1, 0, 2).reshape(span, radix * width),
    )
    result = exact_dot(inner_cos.T, real) - exact_dot(inner_sin.T, imag)
    return (result / order).reshape(length, width)


def sum_shares(share, axis):
    count = lax.axis_size(axis)
    rank = lax.axis_index(axis)
    columns = share.shape[1] // count
    total = lax.dynamic_slice_in_dim(share, rank * columns, columns, axis=1)
    for step in range(1, count):
        piece = lax.dynamic_slice_in_dim(share, (rank + step) % count * columns, columns, axis=1)
        pairs = [(i, (i + step) % count) for i in range(count)]
        total = total + lax.ppermute(piece.astype(jnp.bfloat16), axis, pairs).astype(jnp.float32)
    return total


def shards(query, key_in, value, short_taps, skip_gain, filter_spectrum, out_weight):
    devices = lax.axis_size("ctx")
    tokens, channels = query.shape
    length, block = tokens * devices, channels // devices
    tails = shifted_in(jnp.concatenate([query[-2:], key_in[-2:], value[-2:]], axis=0), "ctx")
    gate_signal = causal_filter(query, tails[0:2], short_taps[0])
    mixed_in = causal_filter(key_in, tails[2:4], short_taps[1]) * causal_filter(
        value, tails[4:6], short_taps[2]
    )
    own_signal = mixed_in.astype(jnp.bfloat16).reshape(tokens, devices, block).transpose(1, 0, 2)
    own_spectrum = (
        filter_spectrum.astype(jnp.bfloat16)
        .reshape(tokens, 2, 2, devices, block)
        .transpose(3, 2, 0, 1, 4)
        .reshape(devices, 4 * tokens, block)
    )
    sent = jnp.concatenate([own_signal, own_spectrum], axis=1)
    taken = lax.all_to_all(sent, "ctx", split_axis=0, concat_axis=0, tiled=True)
    signal = taken[:, :tokens].reshape(length, block)
    spectrum_real = taken[:, tokens : 3 * tokens].reshape(2 * length, block)
    spectrum_imag = taken[:, 3 * tokens :].reshape(2 * length, block)
    convolved = long_filter(signal, spectrum_real, spectrum_imag).astype(jnp.bfloat16)
    convolved = lax.all_to_all(
        convolved.reshape(devices, tokens, block), "ctx", split_axis=0, concat_axis=0, tiled=True
    )
    convolved = convolved.transpose(1, 0, 2).reshape(tokens, channels).astype(jnp.float32)
    gated = (gate_signal * (convolved + skip_gain * mixed_in)).astype(jnp.bfloat16)
    share = jnp.dot(gated, out_weight, preferred_element_type=jnp.float32)
    return sum_shares(share, "tp").astype(jnp.bfloat16)


def solution(mesh):
    return jax.shard_map(
        shards,
        mesh=mesh,
        in_specs=(
            P("ctx", "tp"),
            P("ctx", "tp"),
            P("ctx", "tp"),
            P(None, None, "tp"),
            P("tp"),
            P("ctx", None, None, "tp"),
            P("tp", None),
        ),
        out_specs=P("ctx", "tp"),
        check_vma=False,
    )
```

```python
import math

import jax
import jax.numpy as jnp
from jax import lax
from jax.experimental import pallas as pl
from jax.experimental.pallas import tpu as pltpu
from jax.sharding import PartitionSpec as P

RADIX = 8
ROWS = 16
LANES = 128


def shifted_in(rows, axis):
    count = lax.axis_size(axis)
    return lax.ppermute(rows, axis, [(i, i + 1) for i in range(count - 1)])


def causal_filter(signal, tail, taps):
    values = jnp.concatenate([tail, signal], axis=0).astype(jnp.float32)
    return taps[0] * values[2:] + taps[1] * values[1:-1] + taps[2] * values[:-2]


def turn(rows, columns, order):
    index = rows[:, None] * columns[None, :] % order
    angle = (2.0 * math.pi / order) * index.astype(jnp.float32)
    return jnp.cos(angle), jnp.sin(angle)


def exact_dot(left, right):
    return jnp.dot(left, right, precision=lax.Precision.HIGHEST, preferred_element_type=jnp.float32)


def radix_of(order):
    return 2 ** ((order.bit_length() - 1) // 2)


def long_filter(signal, spectrum_real, spectrum_imag):
    length, width = signal.shape
    order = spectrum_real.shape[0]
    radix = radix_of(order)
    span, depth = order // radix, length // radix
    low = jnp.arange(span, dtype=jnp.int32)
    deep = jnp.arange(depth, dtype=jnp.int32)
    lanes = jnp.arange(radix, dtype=jnp.int32)
    inner_cos, inner_sin = turn(low, deep, span)
    twiddle_cos, twiddle_sin = (t[:, :, None] for t in turn(lanes, low, order))
    outer_cos, outer_sin = turn(lanes, lanes, radix)

    samples = signal.astype(jnp.float32).reshape(depth, radix * width)
    real = exact_dot(inner_cos, samples).reshape(span, radix, width).transpose(1, 0, 2)
    imag = -exact_dot(inner_sin, samples).reshape(span, radix, width).transpose(1, 0, 2)
    real, imag = (
        (real * twiddle_cos + imag * twiddle_sin).reshape(radix, span * width),
        (imag * twiddle_cos - real * twiddle_sin).reshape(radix, span * width),
    )
    real, imag = (
        exact_dot(outer_cos, real) + exact_dot(outer_sin, imag),
        exact_dot(outer_cos, imag) - exact_dot(outer_sin, real),
    )
    spectrum_real = spectrum_real.astype(jnp.float32).reshape(radix, span * width)
    spectrum_imag = spectrum_imag.astype(jnp.float32).reshape(radix, span * width)
    real, imag = (
        real * spectrum_real - imag * spectrum_imag,
        real * spectrum_imag + imag * spectrum_real,
    )
    real, imag = (
        (exact_dot(outer_cos, real) - exact_dot(outer_sin, imag)).reshape(radix, span, width),
        (exact_dot(outer_cos, imag) + exact_dot(outer_sin, real)).reshape(radix, span, width),
    )
    real, imag = (
        (real * twiddle_cos - imag * twiddle_sin).transpose(1, 0, 2).reshape(span, radix * width),
        (imag * twiddle_cos + real * twiddle_sin).transpose(1, 0, 2).reshape(span, radix * width),
    )
    result = exact_dot(inner_cos.T, real) - exact_dot(inner_sin.T, imag)
    return (result / order).reshape(length, width)


def split(value):
    high = value.astype(jnp.bfloat16)
    return high, (value - high.astype(jnp.float32)).astype(jnp.bfloat16)


def butterfly(parts, sign):
    count = len(parts)
    if count == 1:
        return parts
    even, odd = butterfly(parts[0::2], sign), butterfly(parts[1::2], sign)
    half = count // 2
    low, high = [], []
    for j in range(half):
        real, imag = odd[j]
        if 4 * j == count:
            real, imag = (-imag, real) if sign > 0 else (imag, -real)
        elif j:
            c, s = math.cos(2.0 * math.pi * j / count), sign * math.sin(2.0 * math.pi * j / count)
            if 8 * j == count:
                real, imag = ((real - imag) * c, (real + imag) * c) if sign > 0 else ((real + imag) * c, (imag - real) * c)
            elif 8 * j == 3 * count:
                real, imag = ((real + imag) * c, (imag - real) * c) if sign > 0 else ((real - imag) * c, (real + imag) * c)
            else:
                real, imag = real * c - imag * s, real * s + imag * c
        low.append((even[j][0] + real, even[j][1] + imag))
        high.append((even[j][0] - real, even[j][1] - imag))
    return low + high


def transform_kernel(
    taken_ref, fwd_high, fwd_low, inv_high, inv_low, cos_ref, sin_ref, out_ref,
    samples, packed, inner, high_ref, low_ref,
):
    devices, tokens, block = out_ref.shape
    span = cos_ref.shape[1]
    depth = packed.shape[0]
    per_source = 2 * tokens

    for q in range(devices):
        samples[pl.ds(q * tokens, tokens), :] = taken_ref[q, pl.ds(0, tokens), :].astype(jnp.float32)
    for v in range(RADIX):
        packed[:, pl.ds(v * block, block)] = samples[pl.ds(v, depth, stride=RADIX), :].astype(jnp.bfloat16)

    wide = 2 * block

    @pl.loop(0, RADIX * block // wide)
    def _(i):
        lanes = pl.ds(pl.multiple_of(i * wide, wide), wide)
        right = packed[:, lanes]
        inner[:, lanes] = jnp.dot(fwd_high[...], right, preferred_element_type=jnp.float32) + jnp.dot(
            fwd_low[...], right, preferred_element_type=jnp.float32
        )

    @pl.loop(0, span // ROWS)
    def _(i):
        start = pl.multiple_of(i * ROWS, ROWS)
        rows, rows_imag = pl.ds(start, ROWS), pl.ds(pl.multiple_of(start + span, ROWS), ROWS)
        parts = []
        for v in range(RADIX):
            lanes = pl.ds(v * block, block)
            real, imag = inner[rows, lanes], inner[rows_imag, lanes]
            if v:
                c, s = cos_ref[v, rows, :], sin_ref[v, rows, :]
                real, imag = real * c - imag * s, -(imag * c + real * s)
            else:
                imag = -imag
            parts.append((real, imag))
        parts = butterfly(parts, -1)
        scaled = []
        for j in range(RADIX):
            place = start + j * span
            source, row = place // per_source, place % per_source
            real_rows = pl.ds(pl.multiple_of(tokens + row, ROWS), ROWS)
            imag_rows = pl.ds(pl.multiple_of(tokens + per_source + row, ROWS), ROWS)
            fr = taken_ref[source, real_rows, :].astype(jnp.float32)
            fi = taken_ref[source, imag_rows, :].astype(jnp.float32)
            real, imag = parts[j]
            scaled.append((real * fr - imag * fi, real * fi + imag * fr))
        parts = butterfly(scaled, 1)
        for v in range(RADIX):
            lanes = pl.ds(v * block, block)
            real, imag = parts[v]
            if v:
                c, s = cos_ref[v, rows, :], sin_ref[v, rows, :]
                real, imag = real * c - imag * s, imag * c + real * s
            high_ref[rows, lanes], low_ref[rows, lanes] = split(real)
            high_ref[rows_imag, lanes], low_ref[rows_imag, lanes] = split(-imag)

    for v in range(0, RADIX, 2):
        lanes = pl.ds(v * block, wide)
        right = high_ref[:, lanes]
        result = (
            jnp.dot(inv_high[...], right, preferred_element_type=jnp.float32)
            + jnp.dot(inv_low[...], right, preferred_element_type=jnp.float32)
            + jnp.dot(inv_high[...], low_ref[:, lanes], preferred_element_type=jnp.float32)
        ) * (0.5 / (devices * tokens))
        samples[pl.ds(v, depth, stride=RADIX), :] = result[:, :block]
        samples[pl.ds(v + 1, depth, stride=RADIX), :] = result[:, block:]
    for q in range(devices):
        out_ref[q, :, :] = samples[pl.ds(q * tokens, tokens), :].astype(jnp.bfloat16)


def local_tables(length, block):
    order = 2 * length
    span, depth = order // RADIX, length // RADIX
    low, deep, lanes = lax.optimization_barrier(
        tuple(jnp.arange(size, dtype=jnp.int32) for size in (span, depth, RADIX))
    )
    forward = jnp.concatenate(turn(low, deep, span), axis=0)
    inverse = jnp.concatenate(turn(deep, low, span), axis=1)
    twiddles = tuple(
        jnp.broadcast_to(t[:, :, None], (RADIX, span, block)) for t in turn(lanes, low, order)
    )
    return (*split(forward), *split(inverse), *twiddles)


def local_transform(taken, tables, tokens):
    devices, _, block = taken.shape
    length = devices * tokens
    span, depth = 2 * length // RADIX, length // RADIX
    flops = 5 * 2 * 2 * span * depth * RADIX * block
    return pl.pallas_call(
        transform_kernel,
        out_shape=jax.ShapeDtypeStruct((devices, tokens, block), jnp.bfloat16),
        in_specs=[pl.BlockSpec(memory_space=pltpu.VMEM)] * 7,
        out_specs=pl.BlockSpec(memory_space=pltpu.VMEM),
        scratch_shapes=[
            pltpu.VMEM((length, block), jnp.float32),
            pltpu.VMEM((depth, RADIX * block), jnp.bfloat16),
            pltpu.VMEM((2 * span, RADIX * block), jnp.float32),
            pltpu.VMEM((2 * span, RADIX * block), jnp.bfloat16),
            pltpu.VMEM((2 * span, RADIX * block), jnp.bfloat16),
        ],
        compiler_params=pltpu.CompilerParams(vmem_limit_bytes=40 * 2**20),
        cost_estimate=pl.CostEstimate(flops=flops, bytes_accessed=taken.size * 2, transcendentals=0),
    )(taken, *tables)


def sum_shares(share, axis):
    count = lax.axis_size(axis)
    rank = lax.axis_index(axis)
    columns = share.shape[1] // count
    total = lax.dynamic_slice_in_dim(share, rank * columns, columns, axis=1)
    for step in range(1, count):
        piece = lax.dynamic_slice_in_dim(share, (rank + step) % count * columns, columns, axis=1)
        pairs = [(i, (i + step) % count) for i in range(count)]
        total = total + lax.ppermute(piece.astype(jnp.bfloat16), axis, pairs).astype(jnp.float32)
    return total


def shards(query, key_in, value, short_taps, skip_gain, filter_spectrum, out_weight):
    devices = lax.axis_size("ctx")
    tokens, channels = query.shape
    length, block = tokens * devices, channels // devices
    tails = shifted_in(jnp.concatenate([query[-2:], key_in[-2:], value[-2:]], axis=0), "ctx")
    gate_signal = causal_filter(query, tails[0:2], short_taps[0])
    mixed_in = causal_filter(key_in, tails[2:4], short_taps[1]) * causal_filter(
        value, tails[4:6], short_taps[2]
    )
    own_signal = mixed_in.astype(jnp.bfloat16).reshape(tokens, devices, block).transpose(1, 0, 2)
    own_spectrum = (
        filter_spectrum.astype(jnp.bfloat16)
        .reshape(tokens, 2, 2, devices, block)
        .transpose(3, 2, 0, 1, 4)
        .reshape(devices, 4 * tokens, block)
    )
    sent = jnp.concatenate([own_signal, own_spectrum], axis=1)
    taken = lax.all_to_all(sent, "ctx", split_axis=0, concat_axis=0, tiled=True)
    if block == LANES:
        convolved = local_transform(taken, local_tables(length, block), tokens)
    else:
        signal = taken[:, :tokens].reshape(length, block)
        spectrum_real = taken[:, tokens : 3 * tokens].reshape(2 * length, block)
        spectrum_imag = taken[:, 3 * tokens :].reshape(2 * length, block)
        convolved = long_filter(signal, spectrum_real, spectrum_imag).astype(jnp.bfloat16)
    convolved = lax.all_to_all(
        convolved.reshape(devices, tokens, block), "ctx", split_axis=0, concat_axis=0, tiled=True
    )
    convolved = convolved.transpose(1, 0, 2).reshape(tokens, channels).astype(jnp.float32)
    gated = (gate_signal * (convolved + skip_gain * mixed_in)).astype(jnp.bfloat16)
    share = jnp.dot(gated, out_weight, preferred_element_type=jnp.float32)
    return sum_shares(share, "tp").astype(jnp.bfloat16)


def solution(mesh):
    return jax.shard_map(
        shards,
        mesh=mesh,
        in_specs=(
            P("ctx", "tp"),
            P("ctx", "tp"),
            P("ctx", "tp"),
            P(None, None, "tp"),
            P("tp"),
            P("ctx", None, None, "tp"),
            P("tp", None),
        ),
        out_specs=P("ctx", "tp"),
        check_vma=False,
    )
```

```python
import math

import jax
import jax.numpy as jnp
from jax import lax
from jax.experimental import pallas as pl
from jax.experimental.pallas import tpu as pltpu
from jax.sharding import PartitionSpec as P

RADIX = 8
ROWS = 16
LANES = 128
WIDTH = 512


def shifted_in(rows, axis):
    count = lax.axis_size(axis)
    return lax.ppermute(rows, axis, [(i, i + 1) for i in range(count - 1)])


def causal_filter(signal, tail, taps):
    values = jnp.concatenate([tail, signal], axis=0).astype(jnp.float32)
    return taps[0] * values[2:] + taps[1] * values[1:-1] + taps[2] * values[:-2]


def turn(rows, columns, order):
    index = rows[:, None] * columns[None, :] % order
    angle = (2.0 * math.pi / order) * index.astype(jnp.float32)
    return jnp.cos(angle), jnp.sin(angle)


def exact_dot(left, right):
    return jnp.dot(left, right, precision=lax.Precision.HIGHEST, preferred_element_type=jnp.float32)


def radix_of(order):
    return 2 ** ((order.bit_length() - 1) // 2)


def long_filter(signal, spectrum_real, spectrum_imag):
    length, width = signal.shape
    order = spectrum_real.shape[0]
    radix = radix_of(order)
    span, depth = order // radix, length // radix
    low = jnp.arange(span, dtype=jnp.int32)
    deep = jnp.arange(depth, dtype=jnp.int32)
    lanes = jnp.arange(radix, dtype=jnp.int32)
    inner_cos, inner_sin = turn(low, deep, span)
    twiddle_cos, twiddle_sin = (t[:, :, None] for t in turn(lanes, low, order))
    outer_cos, outer_sin = turn(lanes, lanes, radix)

    samples = signal.astype(jnp.float32).reshape(depth, radix * width)
    real = exact_dot(inner_cos, samples).reshape(span, radix, width).transpose(1, 0, 2)
    imag = -exact_dot(inner_sin, samples).reshape(span, radix, width).transpose(1, 0, 2)
    real, imag = (
        (real * twiddle_cos + imag * twiddle_sin).reshape(radix, span * width),
        (imag * twiddle_cos - real * twiddle_sin).reshape(radix, span * width),
    )
    real, imag = (
        exact_dot(outer_cos, real) + exact_dot(outer_sin, imag),
        exact_dot(outer_cos, imag) - exact_dot(outer_sin, real),
    )
    spectrum_real = spectrum_real.astype(jnp.float32).reshape(radix, span * width)
    spectrum_imag = spectrum_imag.astype(jnp.float32).reshape(radix, span * width)
    real, imag = (
        real * spectrum_real - imag * spectrum_imag,
        real * spectrum_imag + imag * spectrum_real,
    )
    real, imag = (
        (exact_dot(outer_cos, real) - exact_dot(outer_sin, imag)).reshape(radix, span, width),
        (exact_dot(outer_cos, imag) + exact_dot(outer_sin, real)).reshape(radix, span, width),
    )
    real, imag = (
        (real * twiddle_cos - imag * twiddle_sin).transpose(1, 0, 2).reshape(span, radix * width),
        (imag * twiddle_cos + real * twiddle_sin).transpose(1, 0, 2).reshape(span, radix * width),
    )
    result = exact_dot(inner_cos.T, real) - exact_dot(inner_sin.T, imag)
    return (result / order).reshape(length, width)


def split(value):
    high = value.astype(jnp.bfloat16)
    return high, (value - high.astype(jnp.float32)).astype(jnp.bfloat16)


def split_table(value):
    high = lax.reduce_precision(value, exponent_bits=8, mantissa_bits=7)
    return high.astype(jnp.bfloat16), (value - high).astype(jnp.bfloat16)


def filtered_block(signal_ref, tails_ref, taps_ref, which, lanes):
    values = signal_ref[:, lanes].astype(jnp.float32)
    tails = tails_ref[:, lanes].astype(jnp.float32)
    older, newer = tails[2 * which : 2 * which + 1], tails[2 * which + 1 : 2 * which + 2]
    row = lax.broadcasted_iota(jnp.int32, values.shape, 0)
    one_back = jnp.where(row == 0, newer, pltpu.roll(values, 1, 0))
    two_back = jnp.where(row == 0, older, jnp.where(row == 1, newer, pltpu.roll(values, 2, 0)))
    taps = taps_ref[which, :, lanes]
    return taps[0:1] * values + taps[1:2] * one_back + taps[2:3] * two_back


def pack_kernel(spectrum_ref, sent_ref, staged):
    pairs, group, _ = spectrum_ref.shape
    tokens = sent_ref.shape[1] - 2 * pairs
    staged[...] = spectrum_ref[...].reshape(staged.shape)
    for d in range(group // 2):
        for r in range(2):
            sent_ref[d, pl.ds(tokens + r * pairs, pairs), :] = staged[
                pl.ds(2 * d + r, pairs, stride=group), :
            ].astype(jnp.bfloat16)


def packed_spectrum(filter_spectrum, devices):
    tokens, _, _, channels = filter_spectrum.shape
    block = channels // devices
    pairs = 2 * tokens
    view = (
        filter_spectrum.reshape(tokens, 2, 2, devices, block)
        .transpose(0, 1, 3, 2, 4)
        .reshape(pairs, 2 * devices, block)
    )
    rows = tokens + 2 * pairs
    return pl.pallas_call(
        pack_kernel,
        grid=(devices // 4,),
        out_shape=jax.ShapeDtypeStruct((devices, rows, block), jnp.bfloat16),
        in_specs=[pl.BlockSpec((pairs, 8, block), lambda i: (0, i, 0))],
        out_specs=pl.BlockSpec((4, rows, block), lambda i: (i, 0, 0)),
        scratch_shapes=[pltpu.VMEM((pairs * 8, block), jnp.float32)],
        compiler_params=pltpu.CompilerParams(vmem_limit_bytes=16 * 2**20),
        cost_estimate=pl.CostEstimate(
            flops=0, bytes_accessed=view.size * 6, transcendentals=0
        ),
    )(view)


def mix_kernel(key_ref, value_ref, tails_ref, taps_ref, _, sent_ref):
    devices, _, block = sent_ref.shape
    for j in range(devices):
        lanes = pl.ds(j * block, block)
        mixed = filtered_block(key_ref, tails_ref, taps_ref, 1, lanes) * filtered_block(
            value_ref, tails_ref, taps_ref, 2, lanes
        )
        sent_ref[j] = mixed.astype(jnp.bfloat16)


def with_signal(key_in, value, tails, short_taps, sent):
    devices, _, block = sent.shape
    tokens = key_in.shape[0]
    whole = pl.BlockSpec(memory_space=pltpu.VMEM)
    return pl.pallas_call(
        mix_kernel,
        grid=(1,),
        out_shape=jax.ShapeDtypeStruct(sent.shape, sent.dtype),
        in_specs=[whole] * 4 + [pl.BlockSpec(memory_space=pl.ANY)],
        out_specs=pl.BlockSpec((devices, tokens, block), lambda i: (0, 0, 0)),
        input_output_aliases={4: 0},
        compiler_params=pltpu.CompilerParams(vmem_limit_bytes=16 * 2**20),
        cost_estimate=pl.CostEstimate(
            flops=12 * key_in.size, bytes_accessed=6 * key_in.size, transcendentals=0
        ),
    )(key_in, value, tails, short_taps, sent)


def gate_kernel(query_ref, key_ref, value_ref, tails_ref, taps_ref, gain_ref, gate_ref, direct_ref):
    tokens, channels = query_ref.shape
    for j in range(channels // LANES):
        lanes = pl.ds(j * LANES, LANES)
        mixed = filtered_block(key_ref, tails_ref, taps_ref, 1, lanes) * filtered_block(
            value_ref, tails_ref, taps_ref, 2, lanes
        )
        gate_ref[:, lanes] = filtered_block(query_ref, tails_ref, taps_ref, 0, lanes)
        direct_ref[:, lanes] = gain_ref[:, lanes] * mixed


def gates(query, key_in, value, tails, short_taps, skip_gain):
    shape = jax.ShapeDtypeStruct(query.shape, jnp.float32)
    whole = pl.BlockSpec(memory_space=pltpu.VMEM)
    return pl.pallas_call(
        gate_kernel,
        out_shape=(shape, shape),
        in_specs=[whole] * 6,
        out_specs=(whole, whole),
        compiler_params=pltpu.CompilerParams(vmem_limit_bytes=16 * 2**20),
        cost_estimate=pl.CostEstimate(
            flops=20 * query.size, bytes_accessed=14 * query.size, transcendentals=0
        ),
    )(query, key_in, value, tails, short_taps, skip_gain[None, :])


def columns_of(rank, count, columns, width):
    return pl.ds(pl.multiple_of(rank * columns + count * width, width), width)


def far_kernel(conv_ref, gate_ref, direct_ref, weight_ref, gated_ref, share_ref):
    devices, _, block = conv_ref.shape
    columns = share_ref.shape[1]
    for j in range(devices):
        lanes = pl.ds(j * block, block)
        gated_ref[:, lanes] = (
            gate_ref[:, lanes] * (conv_ref[j].astype(jnp.float32) + direct_ref[:, lanes])
        ).astype(jnp.bfloat16)
    other = 1 - lax.axis_index("tp")

    @pl.loop(0, columns // WIDTH)
    def _(i):
        place = pl.ds(pl.multiple_of(i * WIDTH, WIDTH), WIDTH)
        share_ref[:, place] = jnp.dot(
            gated_ref[...],
            weight_ref[:, columns_of(other, i, columns, WIDTH)],
            preferred_element_type=jnp.float32,
        ).astype(jnp.bfloat16)


def near_kernel(gated_ref, weight_ref, share_ref):
    columns = share_ref.shape[1]
    rank = lax.axis_index("tp")

    @pl.loop(0, columns // WIDTH)
    def _(i):
        place = pl.ds(pl.multiple_of(i * WIDTH, WIDTH), WIDTH)
        share_ref[:, place] = jnp.dot(
            gated_ref[...],
            weight_ref[:, columns_of(rank, i, columns, WIDTH)],
            preferred_element_type=jnp.float32,
        )


def projected(convolved, gate_signal, direct, out_weight):
    tokens, channels = gate_signal.shape
    columns = out_weight.shape[1] // 2
    whole = pl.BlockSpec(memory_space=pltpu.VMEM)
    cost = pl.CostEstimate(
        flops=2 * tokens * channels * columns, bytes_accessed=2 * channels * columns, transcendentals=0
    )
    params = pltpu.CompilerParams(vmem_limit_bytes=40 * 2**20)
    gated, far = pl.pallas_call(
        far_kernel,
        out_shape=(
            jax.ShapeDtypeStruct((tokens, channels), jnp.bfloat16),
            jax.ShapeDtypeStruct((tokens, columns), jnp.bfloat16),
        ),
        in_specs=[whole] * 4,
        out_specs=(whole, whole),
        compiler_params=params,
        cost_estimate=cost,
    )(convolved, gate_signal, direct, out_weight)
    arrived = lax.ppermute(far, "tp", [(0, 1), (1, 0)])
    near = pl.pallas_call(
        near_kernel,
        out_shape=jax.ShapeDtypeStruct((tokens, columns), jnp.float32),
        in_specs=[whole] * 2,
        out_specs=whole,
        compiler_params=params,
        cost_estimate=cost,
    )(gated, out_weight)
    return (near + arrived.astype(jnp.float32)).astype(jnp.bfloat16)


def butterfly(parts, sign):
    count = len(parts)
    if count == 1:
        return parts
    even, odd = butterfly(parts[0::2], sign), butterfly(parts[1::2], sign)
    half = count // 2
    low, high = [], []
    for j in range(half):
        real, imag = odd[j]
        if 4 * j == count:
            real, imag = (-imag, real) if sign > 0 else (imag, -real)
        elif j:
            c, s = math.cos(2.0 * math.pi * j / count), sign * math.sin(2.0 * math.pi * j / count)
            if 8 * j == count:
                real, imag = ((real - imag) * c, (real + imag) * c) if sign > 0 else ((real + imag) * c, (imag - real) * c)
            elif 8 * j == 3 * count:
                real, imag = ((real + imag) * c, (imag - real) * c) if sign > 0 else ((real - imag) * c, (real + imag) * c)
            else:
                real, imag = real * c - imag * s, real * s + imag * c
        low.append((even[j][0] + real, even[j][1] + imag))
        high.append((even[j][0] - real, even[j][1] - imag))
    return low + high


def transform_kernel(
    taken_ref, fwd_high, fwd_low, inv_high, inv_low, cos_ref, sin_ref, out_ref,
    samples, packed, inner, high_ref, low_ref,
):
    devices, tokens, block = out_ref.shape
    span = cos_ref.shape[1]
    depth = packed.shape[0]
    per_source = 2 * tokens

    for q in range(devices):
        samples[pl.ds(q * tokens, tokens), :] = taken_ref[q, pl.ds(0, tokens), :].astype(jnp.float32)
    for v in range(RADIX):
        packed[:, pl.ds(v * block, block)] = samples[pl.ds(v, depth, stride=RADIX), :].astype(jnp.bfloat16)

    wide = 2 * block

    @pl.loop(0, RADIX * block // wide)
    def _(i):
        lanes = pl.ds(pl.multiple_of(i * wide, wide), wide)
        right = packed[:, lanes]
        inner[:, lanes] = jnp.dot(fwd_high[...], right, preferred_element_type=jnp.float32) + jnp.dot(
            fwd_low[...], right, preferred_element_type=jnp.float32
        )

    @pl.loop(0, span // ROWS)
    def _(i):
        start = pl.multiple_of(i * ROWS, ROWS)
        rows, rows_imag = pl.ds(start, ROWS), pl.ds(pl.multiple_of(start + span, ROWS), ROWS)
        parts = []
        for v in range(RADIX):
            lanes = pl.ds(v * block, block)
            real, imag = inner[rows, lanes], inner[rows_imag, lanes]
            if v:
                c, s = cos_ref[v, rows, :], sin_ref[v, rows, :]
                real, imag = real * c - imag * s, -(imag * c + real * s)
            else:
                imag = -imag
            parts.append((real, imag))
        parts = butterfly(parts, -1)
        scaled = []
        for j in range(RADIX):
            place = start + j * span
            source, row = place // per_source, place % per_source
            real_rows = pl.ds(pl.multiple_of(tokens + row, ROWS), ROWS)
            imag_rows = pl.ds(pl.multiple_of(tokens + per_source + row, ROWS), ROWS)
            fr = taken_ref[source, real_rows, :].astype(jnp.float32)
            fi = taken_ref[source, imag_rows, :].astype(jnp.float32)
            real, imag = parts[j]
            scaled.append((real * fr - imag * fi, real * fi + imag * fr))
        parts = butterfly(scaled, 1)
        for v in range(RADIX):
            lanes = pl.ds(v * block, block)
            real, imag = parts[v]
            if v:
                c, s = cos_ref[v, rows, :], sin_ref[v, rows, :]
                real, imag = real * c - imag * s, imag * c + real * s
            high_ref[rows, lanes], low_ref[rows, lanes] = split(real)
            high_ref[rows_imag, lanes], low_ref[rows_imag, lanes] = split(-imag)

    for v in range(0, RADIX, 2):
        lanes = pl.ds(v * block, wide)
        right = high_ref[:, lanes]
        result = (
            jnp.dot(inv_high[...], right, preferred_element_type=jnp.float32)
            + jnp.dot(inv_low[...], right, preferred_element_type=jnp.float32)
            + jnp.dot(inv_high[...], low_ref[:, lanes], preferred_element_type=jnp.float32)
        ) * (0.5 / (devices * tokens))
        samples[pl.ds(v, depth, stride=RADIX), :] = result[:, :block]
        samples[pl.ds(v + 1, depth, stride=RADIX), :] = result[:, block:]
    for q in range(devices):
        out_ref[q, :, :] = samples[pl.ds(q * tokens, tokens), :].astype(jnp.bfloat16)


def local_tables(length, block):
    order = 2 * length
    span, depth = order // RADIX, length // RADIX
    low, deep, lanes = lax.optimization_barrier(
        tuple(jnp.arange(size, dtype=jnp.int32) for size in (span, depth, RADIX))
    )
    forward = jnp.concatenate(turn(low, deep, span), axis=0)
    inverse = jnp.concatenate(turn(deep, low, span), axis=1)
    twiddles = tuple(
        jnp.broadcast_to(t[:, :, None], (RADIX, span, block)) for t in turn(lanes, low, order)
    )
    return (*split_table(forward), *split_table(inverse), *twiddles)


def local_transform(taken, tables, tokens):
    devices, _, block = taken.shape
    length = devices * tokens
    span, depth = 2 * length // RADIX, length // RADIX
    flops = 5 * 2 * 2 * span * depth * RADIX * block
    return pl.pallas_call(
        transform_kernel,
        out_shape=jax.ShapeDtypeStruct((devices, tokens, block), jnp.bfloat16),
        in_specs=[pl.BlockSpec(memory_space=pltpu.VMEM)] * 7,
        out_specs=pl.BlockSpec(memory_space=pltpu.VMEM),
        scratch_shapes=[
            pltpu.VMEM((length, block), jnp.float32),
            pltpu.VMEM((depth, RADIX * block), jnp.bfloat16),
            pltpu.VMEM((2 * span, RADIX * block), jnp.float32),
            pltpu.VMEM((2 * span, RADIX * block), jnp.bfloat16),
            pltpu.VMEM((2 * span, RADIX * block), jnp.bfloat16),
        ],
        compiler_params=pltpu.CompilerParams(vmem_limit_bytes=40 * 2**20),
        cost_estimate=pl.CostEstimate(flops=flops, bytes_accessed=taken.size * 2, transcendentals=0),
    )(taken, *tables)


def sum_shares(share, axis):
    count = lax.axis_size(axis)
    rank = lax.axis_index(axis)
    columns = share.shape[1] // count
    total = lax.dynamic_slice_in_dim(share, rank * columns, columns, axis=1)
    for step in range(1, count):
        piece = lax.dynamic_slice_in_dim(share, (rank + step) % count * columns, columns, axis=1)
        pairs = [(i, (i + step) % count) for i in range(count)]
        total = total + lax.ppermute(piece.astype(jnp.bfloat16), axis, pairs).astype(jnp.float32)
    return total


def fused_shards(query, key_in, value, short_taps, skip_gain, filter_spectrum, out_weight):
    devices = lax.axis_size("ctx")
    tokens, channels = query.shape
    tails = shifted_in(jnp.concatenate([query[-2:], key_in[-2:], value[-2:]], axis=0), "ctx")
    sent = packed_spectrum(filter_spectrum, devices)
    sent = with_signal(key_in, value, tails, short_taps, sent)
    taken = lax.all_to_all(sent, "ctx", split_axis=0, concat_axis=0, tiled=True)
    gate_signal, direct = gates(query, key_in, value, tails, short_taps, skip_gain)
    tables = local_tables(tokens * devices, channels // devices)
    convolved = local_transform(taken, tables, tokens)
    convolved = lax.all_to_all(convolved, "ctx", split_axis=0, concat_axis=0, tiled=True)
    return projected(convolved, gate_signal, direct, out_weight)


def shards(query, key_in, value, short_taps, skip_gain, filter_spectrum, out_weight):
    devices = lax.axis_size("ctx")
    tokens, channels = query.shape
    length, block = tokens * devices, channels // devices
    if block == LANES and devices % 4 == 0 and lax.axis_size("tp") == 2:
        return fused_shards(query, key_in, value, short_taps, skip_gain, filter_spectrum, out_weight)
    tails = shifted_in(jnp.concatenate([query[-2:], key_in[-2:], value[-2:]], axis=0), "ctx")
    gate_signal = causal_filter(query, tails[0:2], short_taps[0])
    mixed_in = causal_filter(key_in, tails[2:4], short_taps[1]) * causal_filter(
        value, tails[4:6], short_taps[2]
    )
    own_signal = mixed_in.astype(jnp.bfloat16).reshape(tokens, devices, block).transpose(1, 0, 2)
    own_spectrum = (
        filter_spectrum.astype(jnp.bfloat16)
        .reshape(tokens, 2, 2, devices, block)
        .transpose(3, 2, 0, 1, 4)
        .reshape(devices, 4 * tokens, block)
    )
    sent = jnp.concatenate([own_signal, own_spectrum], axis=1)
    taken = lax.all_to_all(sent, "ctx", split_axis=0, concat_axis=0, tiled=True)
    signal = taken[:, :tokens].reshape(length, block)
    spectrum_real = taken[:, tokens : 3 * tokens].reshape(2 * length, block)
    spectrum_imag = taken[:, 3 * tokens :].reshape(2 * length, block)
    convolved = long_filter(signal, spectrum_real, spectrum_imag).astype(jnp.bfloat16)
    convolved = lax.all_to_all(
        convolved.reshape(devices, tokens, block), "ctx", split_axis=0, concat_axis=0, tiled=True
    )
    convolved = convolved.transpose(1, 0, 2).reshape(tokens, channels).astype(jnp.float32)
    gated = (gate_signal * (convolved + skip_gain * mixed_in)).astype(jnp.bfloat16)
    share = jnp.dot(gated, out_weight, preferred_element_type=jnp.float32)
    return sum_shares(share, "tp").astype(jnp.bfloat16)


def solution(mesh):
    return jax.shard_map(
        shards,
        mesh=mesh,
        in_specs=(
            P("ctx", "tp"),
            P("ctx", "tp"),
            P("ctx", "tp"),
            P(None, None, "tp"),
            P("tp"),
            P("ctx", None, None, "tp"),
            P("tp", None),
        ),
        out_specs=P("ctx", "tp"),
        check_vma=False,
    )
```

```python
import math

import jax
import jax.numpy as jnp
from jax import lax
from jax.experimental import pallas as pl
from jax.experimental.pallas import tpu as pltpu
from jax.sharding import PartitionSpec as P

RADIX = 8
ROWS = 16
LANES = 128
WIDTH = 512


def shifted_in(rows, axis):
    count = lax.axis_size(axis)
    return lax.ppermute(rows, axis, [(i, i + 1) for i in range(count - 1)])


def causal_filter(signal, tail, taps):
    values = jnp.concatenate([tail, signal], axis=0).astype(jnp.float32)
    return taps[0] * values[2:] + taps[1] * values[1:-1] + taps[2] * values[:-2]


def turn(rows, columns, order):
    index = rows[:, None] * columns[None, :] % order
    angle = (2.0 * math.pi / order) * index.astype(jnp.float32)
    return jnp.cos(angle), jnp.sin(angle)


def exact_dot(left, right):
    return jnp.dot(left, right, precision=lax.Precision.HIGHEST, preferred_element_type=jnp.float32)


def radix_of(order):
    return 2 ** ((order.bit_length() - 1) // 2)


def long_filter(signal, spectrum_real, spectrum_imag):
    length, width = signal.shape
    order = spectrum_real.shape[0]
    radix = radix_of(order)
    span, depth = order // radix, length // radix
    low = jnp.arange(span, dtype=jnp.int32)
    deep = jnp.arange(depth, dtype=jnp.int32)
    lanes = jnp.arange(radix, dtype=jnp.int32)
    inner_cos, inner_sin = turn(low, deep, span)
    twiddle_cos, twiddle_sin = (t[:, :, None] for t in turn(lanes, low, order))
    outer_cos, outer_sin = turn(lanes, lanes, radix)

    samples = signal.astype(jnp.float32).reshape(depth, radix * width)
    real = exact_dot(inner_cos, samples).reshape(span, radix, width).transpose(1, 0, 2)
    imag = -exact_dot(inner_sin, samples).reshape(span, radix, width).transpose(1, 0, 2)
    real, imag = (
        (real * twiddle_cos + imag * twiddle_sin).reshape(radix, span * width),
        (imag * twiddle_cos - real * twiddle_sin).reshape(radix, span * width),
    )
    real, imag = (
        exact_dot(outer_cos, real) + exact_dot(outer_sin, imag),
        exact_dot(outer_cos, imag) - exact_dot(outer_sin, real),
    )
    spectrum_real = spectrum_real.astype(jnp.float32).reshape(radix, span * width)
    spectrum_imag = spectrum_imag.astype(jnp.float32).reshape(radix, span * width)
    real, imag = (
        real * spectrum_real - imag * spectrum_imag,
        real * spectrum_imag + imag * spectrum_real,
    )
    real, imag = (
        (exact_dot(outer_cos, real) - exact_dot(outer_sin, imag)).reshape(radix, span, width),
        (exact_dot(outer_cos, imag) + exact_dot(outer_sin, real)).reshape(radix, span, width),
    )
    real, imag = (
        (real * twiddle_cos - imag * twiddle_sin).transpose(1, 0, 2).reshape(span, radix * width),
        (imag * twiddle_cos + real * twiddle_sin).transpose(1, 0, 2).reshape(span, radix * width),
    )
    result = exact_dot(inner_cos.T, real) - exact_dot(inner_sin.T, imag)
    return (result / order).reshape(length, width)


def split(value):
    high = value.astype(jnp.bfloat16)
    return high, (value - high.astype(jnp.float32)).astype(jnp.bfloat16)


def split_table(value):
    high = lax.reduce_precision(value, exponent_bits=8, mantissa_bits=7)
    return high.astype(jnp.bfloat16), (value - high).astype(jnp.bfloat16)


def filtered_block(signal_ref, tails_ref, taps_ref, which, lanes):
    values = signal_ref[:, lanes].astype(jnp.float32)
    tails = tails_ref[:, lanes].astype(jnp.float32)
    older, newer = tails[2 * which : 2 * which + 1], tails[2 * which + 1 : 2 * which + 2]
    row = lax.broadcasted_iota(jnp.int32, values.shape, 0)
    one_back = jnp.where(row == 0, newer, pltpu.roll(values, 1, 0))
    two_back = jnp.where(row == 0, older, jnp.where(row == 1, newer, pltpu.roll(values, 2, 0)))
    taps = taps_ref[which, :, lanes]
    return taps[0:1] * values + taps[1:2] * one_back + taps[2:3] * two_back


def tails_kernel(query_ref, key_ref, value_ref, tails_ref):
    rows = query_ref.shape[0]
    for which, ref in enumerate((query_ref, key_ref, value_ref)):
        tails_ref[2 * which : 2 * which + 2, :] = ref[...].astype(jnp.float32)[rows - 2 :].astype(jnp.bfloat16)


def own_tails(query, key_in, value):
    tokens, channels = query.shape
    last = pl.BlockSpec((ROWS, channels), lambda i: (tokens // ROWS - 1, 0))
    return pl.pallas_call(
        tails_kernel,
        grid=(1,),
        out_shape=jax.ShapeDtypeStruct((6, channels), query.dtype),
        in_specs=[last] * 3,
        out_specs=pl.BlockSpec((6, channels), lambda i: (0, 0)),
        compiler_params=pltpu.CompilerParams(vmem_limit_bytes=4 * 2**20),
    )(*(pltpu.with_memory_space_constraint(a, pltpu.HBM) for a in (query, key_in, value)))


def pack_kernel(spectrum_ref, sent_ref, staged):
    pairs, group, _ = spectrum_ref.shape
    tokens = sent_ref.shape[1] - 2 * pairs
    staged[...] = spectrum_ref[...].reshape(staged.shape)
    for d in range(group // 2):
        for r in range(2):
            sent_ref[d, pl.ds(tokens + r * pairs, pairs), :] = staged[
                pl.ds(2 * d + r, pairs, stride=group), :
            ].astype(jnp.bfloat16)


def packed_spectrum(filter_spectrum, devices):
    tokens, _, _, channels = filter_spectrum.shape
    block = channels // devices
    pairs = 2 * tokens
    view = (
        filter_spectrum.reshape(tokens, 2, 2, devices, block)
        .transpose(0, 1, 3, 2, 4)
        .reshape(pairs, 2 * devices, block)
    )
    rows = tokens + 2 * pairs
    view = pltpu.with_memory_space_constraint(view, pltpu.HBM)
    return pl.pallas_call(
        pack_kernel,
        grid=(devices // 4,),
        out_shape=jax.ShapeDtypeStruct((devices, rows, block), jnp.bfloat16),
        in_specs=[pl.BlockSpec((pairs, 8, block), lambda i: (0, i, 0))],
        out_specs=pl.BlockSpec((4, rows, block), lambda i: (i, 0, 0)),
        scratch_shapes=[pltpu.VMEM((pairs * 8, block), jnp.float32)],
        compiler_params=pltpu.CompilerParams(vmem_limit_bytes=16 * 2**20),
        cost_estimate=pl.CostEstimate(
            flops=0, bytes_accessed=view.size * 6, transcendentals=0
        ),
    )(view)


def mix_kernel(key_ref, value_ref, tails_ref, taps_ref, _, sent_ref):
    devices, _, block = sent_ref.shape
    for j in range(devices):
        lanes = pl.ds(j * block, block)
        mixed = filtered_block(key_ref, tails_ref, taps_ref, 1, lanes) * filtered_block(
            value_ref, tails_ref, taps_ref, 2, lanes
        )
        sent_ref[j] = mixed.astype(jnp.bfloat16)


def with_signal(key_in, value, tails, short_taps, sent):
    devices, _, block = sent.shape
    tokens = key_in.shape[0]
    whole = pl.BlockSpec(memory_space=pltpu.VMEM)
    return pl.pallas_call(
        mix_kernel,
        grid=(1,),
        out_shape=jax.ShapeDtypeStruct(sent.shape, sent.dtype),
        in_specs=[whole] * 4 + [pl.BlockSpec(memory_space=pl.ANY)],
        out_specs=pl.BlockSpec((devices, tokens, block), lambda i: (0, 0, 0)),
        input_output_aliases={4: 0},
        compiler_params=pltpu.CompilerParams(vmem_limit_bytes=16 * 2**20),
        cost_estimate=pl.CostEstimate(
            flops=12 * key_in.size, bytes_accessed=6 * key_in.size, transcendentals=0
        ),
    )(key_in, value, tails, short_taps, sent)


def gate_kernel(query_ref, key_ref, value_ref, tails_ref, taps_ref, gain_ref, gate_ref, direct_ref):
    tokens, channels = query_ref.shape
    for j in range(channels // LANES):
        lanes = pl.ds(j * LANES, LANES)
        mixed = filtered_block(key_ref, tails_ref, taps_ref, 1, lanes) * filtered_block(
            value_ref, tails_ref, taps_ref, 2, lanes
        )
        gate_ref[:, lanes] = filtered_block(query_ref, tails_ref, taps_ref, 0, lanes)
        direct_ref[:, lanes] = gain_ref[:, lanes] * mixed


def gates(query, key_in, value, tails, short_taps, skip_gain):
    shape = jax.ShapeDtypeStruct(query.shape, jnp.float32)
    whole = pl.BlockSpec(memory_space=pltpu.VMEM)
    return pl.pallas_call(
        gate_kernel,
        out_shape=(shape, shape),
        in_specs=[whole] * 6,
        out_specs=(whole, whole),
        compiler_params=pltpu.CompilerParams(vmem_limit_bytes=16 * 2**20),
        cost_estimate=pl.CostEstimate(
            flops=20 * query.size, bytes_accessed=14 * query.size, transcendentals=0
        ),
    )(query, key_in, value, tails, short_taps, skip_gain[None, :])


def chunk_copies(weight_ref, held, sems, rank):
    chunks, _, width = held.shape
    return [
        pltpu.make_async_copy(
            weight_ref.at[:, pl.ds(pl.multiple_of((rank * chunks + i) * width, width), width)],
            held.at[i],
            sems.at[i],
        )
        for i in range(chunks)
    ]


def far_kernel(conv_ref, gate_ref, direct_ref, weight_ref, gated_ref, share_ref, held, sems):
    devices, _, block = conv_ref.shape
    copies = chunk_copies(weight_ref, held, sems, 1 - lax.axis_index("tp"))
    for copy in copies:
        copy.start()
    for j in range(devices):
        lanes = pl.ds(j * block, block)
        gated_ref[:, lanes] = (
            gate_ref[:, lanes] * (conv_ref[j].astype(jnp.float32) + direct_ref[:, lanes])
        ).astype(jnp.bfloat16)
    for i, copy in enumerate(copies):
        copy.wait()
        share_ref[:, pl.ds(i * WIDTH, WIDTH)] = jnp.dot(
            gated_ref[...], held[i], preferred_element_type=jnp.float32
        ).astype(jnp.bfloat16)


def near_kernel(gated_ref, weight_ref, share_ref, held, sems):
    copies = chunk_copies(weight_ref, held, sems, lax.axis_index("tp"))
    for copy in copies:
        copy.start()
    for i, copy in enumerate(copies):
        copy.wait()
        share_ref[:, pl.ds(i * WIDTH, WIDTH)] = jnp.dot(
            gated_ref[...], held[i], preferred_element_type=jnp.float32
        )


def projected(convolved, gate_signal, direct, out_weight):
    tokens, channels = gate_signal.shape
    columns = out_weight.shape[1] // 2
    whole = pl.BlockSpec(memory_space=pltpu.VMEM)
    cost = pl.CostEstimate(
        flops=2 * tokens * channels * columns, bytes_accessed=2 * channels * columns, transcendentals=0
    )
    common = {
        "scratch_shapes": [
            pltpu.VMEM((columns // WIDTH, channels, WIDTH), jnp.bfloat16),
            pltpu.SemaphoreType.DMA((columns // WIDTH,)),
        ],
        "compiler_params": pltpu.CompilerParams(vmem_limit_bytes=20 * 2**20),
        "cost_estimate": cost,
    }
    out_weight = pltpu.with_memory_space_constraint(out_weight, pltpu.HBM)
    remote = pl.BlockSpec(memory_space=pltpu.HBM)
    gated, far = pl.pallas_call(
        far_kernel,
        out_shape=(
            jax.ShapeDtypeStruct((tokens, channels), jnp.bfloat16),
            jax.ShapeDtypeStruct((tokens, columns), jnp.bfloat16),
        ),
        in_specs=[whole] * 3 + [remote],
        out_specs=(whole, whole),
        **common,
    )(convolved, gate_signal, direct, out_weight)
    arrived = lax.ppermute(far, "tp", [(0, 1), (1, 0)])
    near = pl.pallas_call(
        near_kernel,
        out_shape=jax.ShapeDtypeStruct((tokens, columns), jnp.float32),
        in_specs=[whole, remote],
        out_specs=whole,
        **common,
    )(gated, out_weight)
    return (near + arrived.astype(jnp.float32)).astype(jnp.bfloat16)


def butterfly(parts, sign):
    count = len(parts)
    if count == 1:
        return parts
    even, odd = butterfly(parts[0::2], sign), butterfly(parts[1::2], sign)
    half = count // 2
    low, high = [], []
    for j in range(half):
        real, imag = odd[j]
        if 4 * j == count:
            real, imag = (-imag, real) if sign > 0 else (imag, -real)
        elif j:
            c, s = math.cos(2.0 * math.pi * j / count), sign * math.sin(2.0 * math.pi * j / count)
            if 8 * j == count:
                real, imag = ((real - imag) * c, (real + imag) * c) if sign > 0 else ((real + imag) * c, (imag - real) * c)
            elif 8 * j == 3 * count:
                real, imag = ((real + imag) * c, (imag - real) * c) if sign > 0 else ((real - imag) * c, (real + imag) * c)
            else:
                real, imag = real * c - imag * s, real * s + imag * c
        low.append((even[j][0] + real, even[j][1] + imag))
        high.append((even[j][0] - real, even[j][1] - imag))
    return low + high


def turned(pair, cosine, sine):
    real, imag = pair
    return real * cosine - imag * sine, imag * cosine + real * sine


def scaled(pair, factor):
    return turned(pair, *factor)


def transform_kernel(
    taken_ref, *refs,
):
    tables, out_ref = refs[:6], refs[6]
    samples, packed, inner, flipped, high_ref, low_ref, done, sem = refs[7:15]
    held, table_sems = refs[15:21], refs[21]
    fwd_high, fwd_low, inv_high, inv_low, cos_ref, sin_ref = held
    loads = [pltpu.make_async_copy(*p, table_sems.at[i]) for i, p in enumerate(zip(tables, held))]
    for load in loads:
        load.start()
    devices, tokens, block = done.shape
    depth = packed.shape[0]
    half = cos_ref.shape[1]
    lane = [pl.ds(v * block, block) for v in range(RADIX)]
    spectrum_real, spectrum_imag = pl.ds(tokens, half), pl.ds(tokens + half, half)

    for q in range(devices):
        samples[pl.ds(q * tokens, tokens), :] = taken_ref[q, pl.ds(0, tokens), :].astype(jnp.float32)
    for v in range(RADIX):
        packed[:, lane[v]] = samples[pl.ds(v, depth, stride=RADIX), :].astype(jnp.bfloat16)

    wide = 2 * block
    loads[0].wait()
    loads[1].wait()
    for v in range(0, RADIX, 2):
        lanes = pl.ds(v * block, wide)
        right = packed[:, lanes]
        inner[:, lanes] = jnp.dot(fwd_high[...], right, preferred_element_type=jnp.float32) + jnp.dot(
            fwd_low[...], right, preferred_element_type=jnp.float32
        )

    row = lax.broadcasted_iota(jnp.int32, (half, half), 0)
    column = lax.broadcasted_iota(jnp.int32, (half, half), 1)
    flip = jnp.where(row + column == half, 1.0, 0.0).astype(jnp.bfloat16)
    for j in range(RADIX):
        source = 2 * RADIX - 1 - 2 * j
        right = jnp.concatenate(
            [taken_ref[source, spectrum_real, :], taken_ref[source, spectrum_imag, :]], axis=1
        )
        flipped[j] = jnp.dot(flip, right, preferred_element_type=jnp.float32).astype(jnp.bfloat16)

    def products(rows, start, parts):
        parts = butterfly(parts, -1)
        result = []
        for j in range(RADIX):
            real = taken_ref[2 * j, pl.ds(start + tokens, ROWS), :].astype(jnp.float32)
            imag = taken_ref[2 * j, pl.ds(start + tokens + half, ROWS), :].astype(jnp.float32)
            mirror = flipped[j, rows, :].astype(jnp.float32)
            result.append(scaled(parts[j], (real + mirror[:, :block], imag - mirror[:, block:])))
        return butterfly(result, 1)

    def middle(start, first):
        rows = pl.ds(start, ROWS)
        rows_imag = pl.ds(start + half, ROWS)
        top = lax.broadcasted_iota(jnp.int32, (ROWS, block), 0) == 0
        parts, tops = [], []
        for v in range(RADIX):
            real, imag = inner[rows, lane[v]], -inner[rows_imag, lane[v]]
            if first:
                tops.append(-imag)
                imag = jnp.where(top, 0.0, imag)
            if v:
                real, imag = turned((real, imag), cos_ref[v, rows, :], -sin_ref[v, rows, :])
            parts.append((real, imag))
        parts = products(rows, start, parts)
        if first:
            angles = [math.pi * v / RADIX for v in range(RADIX)]
            nyquist = [(t * math.cos(a), t * -math.sin(a)) for t, a in zip(tops, angles)]
            nyquist = butterfly(nyquist, -1)
            nyquist = [
                scaled(
                    nyquist[j],
                    (
                        taken_ref[2 * j + 1, pl.ds(tokens, ROWS), :].astype(jnp.float32),
                        taken_ref[2 * j + 1, pl.ds(tokens + half, ROWS), :].astype(jnp.float32),
                    ),
                )
                for j in range(RADIX)
            ]
            nyquist = butterfly(nyquist, 1)
            tops = [n[0] * math.cos(a) - n[1] * math.sin(a) for n, a in zip(nyquist, angles)]
        for v in range(RADIX):
            real, imag = parts[v]
            if v:
                real, imag = turned((real, imag), cos_ref[v, rows, :], sin_ref[v, rows, :])
            imag = jnp.where(top, tops[v], -imag) if first else -imag
            high_ref[rows, lane[v]], low_ref[rows, lane[v]] = split(real)
            high_ref[rows_imag, lane[v]], low_ref[rows_imag, lane[v]] = split(imag)

    for load in loads[2:]:
        load.wait()
    middle(0, True)

    @pl.loop(1, half // ROWS)
    def _(i):
        middle(pl.multiple_of(i * ROWS, ROWS), False)

    for v in range(0, RADIX, 2):
        lanes = pl.ds(v * block, wide)
        right = high_ref[:, lanes]
        result = (
            jnp.dot(inv_high[...], right, preferred_element_type=jnp.float32)
            + jnp.dot(inv_low[...], right, preferred_element_type=jnp.float32)
            + jnp.dot(inv_high[...], low_ref[:, lanes], preferred_element_type=jnp.float32)
        ) * (0.5 / (devices * tokens))
        samples[pl.ds(v, depth, stride=RADIX), :] = result[:, :block]
        samples[pl.ds(v + 1, depth, stride=RADIX), :] = result[:, block:]
    for q in range(devices):
        done[q] = samples[pl.ds(q * tokens, tokens), :].astype(jnp.bfloat16)
    copy = pltpu.make_async_copy(done, out_ref, sem)
    copy.start()
    copy.wait()


def angles_of(shape, rows, columns, order):
    index = lax.broadcasted_iota(jnp.int32, shape, rows) * lax.broadcasted_iota(jnp.int32, shape, columns)
    return (2.0 * math.pi / order) * (index & (order - 1)).astype(jnp.float32)


def tables_kernel(fwd_high, fwd_low, inv_high, inv_low, cos_ref, sin_ref):
    depth = fwd_high.shape[1]
    _, half, block = cos_ref.shape
    order = 2 * RADIX * half

    def alternating(shape, dim):
        return (1 - 2 * (lax.broadcasted_iota(jnp.int32, shape, dim) & 1)).astype(jnp.float32)

    def first(shape, dim):
        return lax.broadcasted_iota(jnp.int32, shape, dim) == 0

    shape = (half, depth)
    angle = angles_of(shape, 0, 1, 2 * half)
    fwd_high[:half], fwd_low[:half] = split(jnp.cos(angle))
    sine = jnp.where(first(shape, 0), alternating(shape, 1), jnp.sin(angle))
    fwd_high[half:], fwd_low[half:] = split(sine)
    shape = (depth, half)
    angle = angles_of(shape, 0, 1, 2 * half)
    inv_high[:, :half], inv_low[:, :half] = split(jnp.cos(angle))
    sine = jnp.where(first(shape, 1), alternating(shape, 0), jnp.sin(angle))
    inv_high[:, half:], inv_low[:, half:] = split(sine)

    for v in range(RADIX):
        step = lax.broadcasted_iota(jnp.int32, (half, block), 0).astype(jnp.float32)
        angle = (2.0 * math.pi * v / order) * step
        cos_ref[v] = jnp.cos(angle)
        sin_ref[v] = jnp.sin(angle)


def local_tables(length, block):
    half, depth = length // RADIX, length // RADIX
    whole = pl.BlockSpec(memory_space=pltpu.VMEM)
    forward = jax.ShapeDtypeStruct((2 * half, depth), jnp.bfloat16)
    inverse = jax.ShapeDtypeStruct((depth, 2 * half), jnp.bfloat16)
    twiddle = jax.ShapeDtypeStruct((RADIX, half, block), jnp.float32)
    return pl.pallas_call(
        tables_kernel,
        out_shape=(forward, forward, inverse, inverse, twiddle, twiddle),
        out_specs=(whole,) * 6,
        compiler_params=pltpu.CompilerParams(vmem_limit_bytes=16 * 2**20),
        cost_estimate=pl.CostEstimate(
            flops=200 * RADIX * half * block, bytes_accessed=8 * RADIX * half * block, transcendentals=0
        ),
    )()


def local_transform(taken, tables, tokens):
    devices, _, block = taken.shape
    length = devices * tokens
    half, depth = length // RADIX, length // RADIX
    flops = 5 * 2 * 2 * half * depth * RADIX * block
    whole, remote = pl.BlockSpec(memory_space=pltpu.VMEM), pl.BlockSpec(memory_space=pltpu.HBM)
    wide = RADIX * block
    tables = [pltpu.with_memory_space_constraint(t, pltpu.HBM) for t in tables]
    return pl.pallas_call(
        transform_kernel,
        out_shape=pltpu.HBM((devices, tokens, block), jnp.bfloat16),
        in_specs=[whole] + [remote] * 6,
        out_specs=remote,
        scratch_shapes=[
            pltpu.VMEM((length, block), jnp.float32),
            pltpu.VMEM((depth, wide), jnp.bfloat16),
            pltpu.VMEM((2 * half, wide), jnp.float32),
            pltpu.VMEM((RADIX, half, 2 * block), jnp.bfloat16),
            pltpu.VMEM((2 * half, wide), jnp.bfloat16),
            pltpu.VMEM((2 * half, wide), jnp.bfloat16),
            pltpu.VMEM((devices, tokens, block), jnp.bfloat16),
            pltpu.SemaphoreType.DMA,
            *(pltpu.VMEM(t.shape, t.dtype) for t in tables),
            pltpu.SemaphoreType.DMA((len(tables),)),
        ],
        compiler_params=pltpu.CompilerParams(vmem_limit_bytes=20 * 2**20),
        cost_estimate=pl.CostEstimate(flops=flops, bytes_accessed=taken.size * 2, transcendentals=0),
    )(taken, *tables)


def sum_shares(share, axis):
    count = lax.axis_size(axis)
    rank = lax.axis_index(axis)
    columns = share.shape[1] // count
    total = lax.dynamic_slice_in_dim(share, rank * columns, columns, axis=1)
    for step in range(1, count):
        piece = lax.dynamic_slice_in_dim(share, (rank + step) % count * columns, columns, axis=1)
        pairs = [(i, (i + step) % count) for i in range(count)]
        total = total + lax.ppermute(piece.astype(jnp.bfloat16), axis, pairs).astype(jnp.float32)
    return total


def fused_shards(query, key_in, value, short_taps, skip_gain, filter_spectrum, out_weight):
    devices = lax.axis_size("ctx")
    tokens, channels = query.shape
    tails = shifted_in(own_tails(query, key_in, value), "ctx")
    sent = packed_spectrum(filter_spectrum, devices)
    sent = with_signal(key_in, value, tails, short_taps, sent)
    taken = lax.all_to_all(sent, "ctx", split_axis=0, concat_axis=0, tiled=True)
    gate_signal, direct = gates(query, key_in, value, tails, short_taps, skip_gain)
    tables = local_tables(tokens * devices, channels // devices)
    convolved = local_transform(taken, tables, tokens)
    convolved = lax.all_to_all(convolved, "ctx", split_axis=0, concat_axis=0, tiled=True)
    return projected(convolved, gate_signal, direct, out_weight)


def shards(query, key_in, value, short_taps, skip_gain, filter_spectrum, out_weight):
    devices = lax.axis_size("ctx")
    tokens, channels = query.shape
    length, block = tokens * devices, channels // devices
    if block == LANES and devices == 2 * RADIX and lax.axis_size("tp") == 2:
        return fused_shards(query, key_in, value, short_taps, skip_gain, filter_spectrum, out_weight)
    tails = shifted_in(jnp.concatenate([query[-2:], key_in[-2:], value[-2:]], axis=0), "ctx")
    gate_signal = causal_filter(query, tails[0:2], short_taps[0])
    mixed_in = causal_filter(key_in, tails[2:4], short_taps[1]) * causal_filter(
        value, tails[4:6], short_taps[2]
    )
    own_signal = mixed_in.astype(jnp.bfloat16).reshape(tokens, devices, block).transpose(1, 0, 2)
    own_spectrum = (
        filter_spectrum.astype(jnp.bfloat16)
        .reshape(tokens, 2, 2, devices, block)
        .transpose(3, 2, 0, 1, 4)
        .reshape(devices, 4 * tokens, block)
    )
    sent = jnp.concatenate([own_signal, own_spectrum], axis=1)
    taken = lax.all_to_all(sent, "ctx", split_axis=0, concat_axis=0, tiled=True)
    signal = taken[:, :tokens].reshape(length, block)
    spectrum_real = taken[:, tokens : 3 * tokens].reshape(2 * length, block)
    spectrum_imag = taken[:, 3 * tokens :].reshape(2 * length, block)
    convolved = long_filter(signal, spectrum_real, spectrum_imag).astype(jnp.bfloat16)
    convolved = lax.all_to_all(
        convolved.reshape(devices, tokens, block), "ctx", split_axis=0, concat_axis=0, tiled=True
    )
    convolved = convolved.transpose(1, 0, 2).reshape(tokens, channels).astype(jnp.float32)
    gated = (gate_signal * (convolved + skip_gain * mixed_in)).astype(jnp.bfloat16)
    share = jnp.dot(gated, out_weight, preferred_element_type=jnp.float32)
    return sum_shares(share, "tp").astype(jnp.bfloat16)


def solution(mesh):
    return jax.shard_map(
        shards,
        mesh=mesh,
        in_specs=(
            P("ctx", "tp"),
            P("ctx", "tp"),
            P("ctx", "tp"),
            P(None, None, "tp"),
            P("tp"),
            P("ctx", None, None, "tp"),
            P("tp", None),
        ),
        out_specs=P("ctx", "tp"),
        check_vma=False,
    )
```

```python
import functools
import math

import jax
import jax.numpy as jnp
from jax import lax
from jax.experimental import pallas as pl
from jax.experimental.pallas import tpu as pltpu
from jax.sharding import PartitionSpec as P

RADIX = 8
ROWS = 16
LANES = 128
WIDTH = 512


def shifted_in(rows, axis):
    count = lax.axis_size(axis)
    return lax.ppermute(rows, axis, [(i, i + 1) for i in range(count - 1)])


def causal_filter(signal, tail, taps):
    values = jnp.concatenate([tail, signal], axis=0).astype(jnp.float32)
    return taps[0] * values[2:] + taps[1] * values[1:-1] + taps[2] * values[:-2]


def turn(rows, columns, order):
    index = rows[:, None] * columns[None, :] % order
    angle = (2.0 * math.pi / order) * index.astype(jnp.float32)
    return jnp.cos(angle), jnp.sin(angle)


def exact_dot(left, right):
    return jnp.dot(left, right, precision=lax.Precision.HIGHEST, preferred_element_type=jnp.float32)


def radix_of(order):
    return 2 ** ((order.bit_length() - 1) // 2)


def long_filter(signal, spectrum_real, spectrum_imag):
    length, width = signal.shape
    order = spectrum_real.shape[0]
    radix = radix_of(order)
    span, depth = order // radix, length // radix
    low = jnp.arange(span, dtype=jnp.int32)
    deep = jnp.arange(depth, dtype=jnp.int32)
    lanes = jnp.arange(radix, dtype=jnp.int32)
    inner_cos, inner_sin = turn(low, deep, span)
    twiddle_cos, twiddle_sin = (t[:, :, None] for t in turn(lanes, low, order))
    outer_cos, outer_sin = turn(lanes, lanes, radix)

    samples = signal.astype(jnp.float32).reshape(depth, radix * width)
    real = exact_dot(inner_cos, samples).reshape(span, radix, width).transpose(1, 0, 2)
    imag = -exact_dot(inner_sin, samples).reshape(span, radix, width).transpose(1, 0, 2)
    real, imag = (
        (real * twiddle_cos + imag * twiddle_sin).reshape(radix, span * width),
        (imag * twiddle_cos - real * twiddle_sin).reshape(radix, span * width),
    )
    real, imag = (
        exact_dot(outer_cos, real) + exact_dot(outer_sin, imag),
        exact_dot(outer_cos, imag) - exact_dot(outer_sin, real),
    )
    spectrum_real = spectrum_real.astype(jnp.float32).reshape(radix, span * width)
    spectrum_imag = spectrum_imag.astype(jnp.float32).reshape(radix, span * width)
    real, imag = (
        real * spectrum_real - imag * spectrum_imag,
        real * spectrum_imag + imag * spectrum_real,
    )
    real, imag = (
        (exact_dot(outer_cos, real) - exact_dot(outer_sin, imag)).reshape(radix, span, width),
        (exact_dot(outer_cos, imag) + exact_dot(outer_sin, real)).reshape(radix, span, width),
    )
    real, imag = (
        (real * twiddle_cos - imag * twiddle_sin).transpose(1, 0, 2).reshape(span, radix * width),
        (imag * twiddle_cos + real * twiddle_sin).transpose(1, 0, 2).reshape(span, radix * width),
    )
    result = exact_dot(inner_cos.T, real) - exact_dot(inner_sin.T, imag)
    return (result / order).reshape(length, width)


def split(value):
    high = value.astype(jnp.bfloat16)
    return high, (value - high.astype(jnp.float32)).astype(jnp.bfloat16)


def split_table(value):
    high = lax.reduce_precision(value, exponent_bits=8, mantissa_bits=7)
    return high.astype(jnp.bfloat16), (value - high).astype(jnp.bfloat16)


def filtered_block(signal_ref, tails_ref, taps_ref, which, lanes):
    values = signal_ref[:, lanes].astype(jnp.float32)
    tails = tails_ref[:, lanes].astype(jnp.float32)
    older, newer = tails[2 * which : 2 * which + 1], tails[2 * which + 1 : 2 * which + 2]
    row = lax.broadcasted_iota(jnp.int32, values.shape, 0)
    one_back = jnp.where(row == 0, newer, pltpu.roll(values, 1, 0))
    two_back = jnp.where(row == 0, older, jnp.where(row == 1, newer, pltpu.roll(values, 2, 0)))
    taps = taps_ref[which, :, lanes]
    return taps[0:1] * values + taps[1:2] * one_back + taps[2:3] * two_back


def tails_kernel(query_ref, key_ref, value_ref, tails_ref):
    rows = query_ref.shape[0]
    for which, ref in enumerate((query_ref, key_ref, value_ref)):
        tails_ref[2 * which : 2 * which + 2, :] = ref[...].astype(jnp.float32)[rows - 2 :].astype(jnp.bfloat16)


def own_tails(query, key_in, value):
    tokens, channels = query.shape
    last = pl.BlockSpec((ROWS, channels), lambda i: (tokens // ROWS - 1, 0))
    return pl.pallas_call(
        tails_kernel,
        grid=(1,),
        out_shape=jax.ShapeDtypeStruct((6, channels), query.dtype),
        in_specs=[last] * 3,
        out_specs=pl.BlockSpec((6, channels), lambda i: (0, 0)),
        compiler_params=pltpu.CompilerParams(vmem_limit_bytes=4 * 2**20),
    )(*(pltpu.with_memory_space_constraint(a, pltpu.HBM) for a in (query, key_in, value)))


def gather_rows(size, count, invert=False):
    row = lax.broadcasted_iota(jnp.int32, (size, size), 0)
    column = lax.broadcasted_iota(jnp.int32, (size, size), 1)
    if invert:
        row, column = column, row
    inner = size // count
    match = column == (row % inner) * count + row // inner
    return jnp.where(match, 1.0, 0.0).astype(jnp.bfloat16)


def exact_rows(matrix, left, right):
    both = jnp.concatenate([left, right], axis=1)
    return jnp.dot(matrix, both, preferred_element_type=jnp.float32).astype(jnp.bfloat16)


def pack_kernel(spectrum_ref, sent_ref):
    pairs, group, block = spectrum_ref.shape
    tokens = sent_ref.shape[1] - 2 * pairs
    part = pairs // group
    matrix = gather_rows(pairs, group)
    slabs = [
        spectrum_ref[pl.ds(k * part, part)].reshape(pairs, block).astype(jnp.bfloat16)
        for k in range(group)
    ]
    for k in range(0, group, 2):
        both = exact_rows(matrix, slabs[k], slabs[k + 1])
        for s in range(group):
            rows = both[s * part : (s + 1) * part]
            start = tokens + (s % 2) * pairs + k * part
            sent_ref[s // 2, pl.ds(start, part), :] = rows[:, :block]
            sent_ref[s // 2, pl.ds(start + part, part), :] = rows[:, block:]


def packed_spectrum(filter_spectrum, devices):
    tokens, _, _, channels = filter_spectrum.shape
    block = channels // devices
    pairs = 2 * tokens
    view = (
        filter_spectrum.reshape(tokens, 2, 2, devices, block)
        .transpose(0, 1, 3, 2, 4)
        .reshape(pairs, 2 * devices, block)
    )
    rows = tokens + 2 * pairs
    view = pltpu.with_memory_space_constraint(view, pltpu.HBM)
    return pl.pallas_call(
        pack_kernel,
        grid=(devices // 4,),
        out_shape=jax.ShapeDtypeStruct((devices, rows, block), jnp.bfloat16),
        in_specs=[pl.BlockSpec((pairs, 8, block), lambda i: (0, i, 0))],
        out_specs=pl.BlockSpec((4, rows, block), lambda i: (i, 0, 0)),
        compiler_params=pltpu.CompilerParams(vmem_limit_bytes=16 * 2**20),
        cost_estimate=pl.CostEstimate(
            flops=0, bytes_accessed=view.size * 6, transcendentals=0
        ),
    )(view)


def mix_kernel(key_ref, value_ref, tails_ref, taps_ref, _, sent_ref):
    devices, _, block = sent_ref.shape
    for j in range(devices):
        lanes = pl.ds(j * block, block)
        mixed = filtered_block(key_ref, tails_ref, taps_ref, 1, lanes) * filtered_block(
            value_ref, tails_ref, taps_ref, 2, lanes
        )
        sent_ref[j] = mixed.astype(jnp.bfloat16)


def with_signal(key_in, value, tails, short_taps, sent):
    devices, _, block = sent.shape
    tokens = key_in.shape[0]
    whole = pl.BlockSpec(memory_space=pltpu.VMEM)
    return pl.pallas_call(
        mix_kernel,
        grid=(1,),
        out_shape=jax.ShapeDtypeStruct(sent.shape, sent.dtype),
        in_specs=[whole] * 4 + [pl.BlockSpec(memory_space=pl.ANY)],
        out_specs=pl.BlockSpec((devices, tokens, block), lambda i: (0, 0, 0)),
        input_output_aliases={4: 0},
        compiler_params=pltpu.CompilerParams(vmem_limit_bytes=16 * 2**20),
        cost_estimate=pl.CostEstimate(
            flops=12 * key_in.size, bytes_accessed=6 * key_in.size, transcendentals=0
        ),
    )(key_in, value, tails, short_taps, sent)


def gate_kernel(query_ref, key_ref, value_ref, tails_ref, taps_ref, gain_ref, gate_ref, direct_ref):
    tokens, channels = query_ref.shape
    for j in range(channels // LANES):
        lanes = pl.ds(j * LANES, LANES)
        mixed = filtered_block(key_ref, tails_ref, taps_ref, 1, lanes) * filtered_block(
            value_ref, tails_ref, taps_ref, 2, lanes
        )
        gate_ref[:, lanes] = filtered_block(query_ref, tails_ref, taps_ref, 0, lanes)
        direct_ref[:, lanes] = gain_ref[:, lanes] * mixed


def gates(query, key_in, value, tails, short_taps, skip_gain):
    shape = jax.ShapeDtypeStruct(query.shape, jnp.float32)
    whole = pl.BlockSpec(memory_space=pltpu.VMEM)
    return pl.pallas_call(
        gate_kernel,
        out_shape=(shape, shape),
        in_specs=[whole] * 6,
        out_specs=(whole, whole),
        compiler_params=pltpu.CompilerParams(vmem_limit_bytes=16 * 2**20),
        cost_estimate=pl.CostEstimate(
            flops=20 * query.size, bytes_accessed=14 * query.size, transcendentals=0
        ),
    )(query, key_in, value, tails, short_taps, skip_gain[None, :])


def chunk_copies(weight_ref, held, sems, first):
    chunks, _, width = held.shape
    return [
        pltpu.make_async_copy(
            weight_ref.at[:, pl.ds(pl.multiple_of((first + i) * width, width), width)],
            held.at[i],
            sems.at[i],
        )
        for i in range(chunks)
    ]


def multiply(gated_ref, share_ref, held, copies):
    width = held.shape[2]
    for i, copy in enumerate(copies):
        copy.wait()
        share_ref[:, pl.ds(i * width, width)] = jnp.dot(
            gated_ref[...], held[i], preferred_element_type=jnp.float32
        ).astype(share_ref.dtype)


def far_kernel(conv_ref, gate_ref, direct_ref, weight_ref, gated_ref, share_ref, held, sems):
    devices, _, block = conv_ref.shape
    chunks = weight_ref.shape[1] // 2 // WIDTH
    copies = chunk_copies(weight_ref, held, sems, (1 - lax.axis_index("tp")) * chunks)
    for copy in copies:
        copy.start()
    for j in range(devices):
        lanes = pl.ds(j * block, block)
        gated_ref[:, lanes] = (
            gate_ref[:, lanes] * (conv_ref[j].astype(jnp.float32) + direct_ref[:, lanes])
        ).astype(jnp.bfloat16)
    multiply(gated_ref, share_ref, held, copies)


def rest_kernel(far, gated_ref, weight_ref, share_ref, held, sems):
    chunks = weight_ref.shape[1] // 2 // WIDTH
    rank = lax.axis_index("tp")
    first = (1 - rank) * chunks + chunks // 2 if far else rank * chunks
    copies = chunk_copies(weight_ref, held, sems, first)
    for copy in copies:
        copy.start()
    multiply(gated_ref, share_ref, held, copies)


def projected(convolved, gate_signal, direct, out_weight):
    tokens, channels = gate_signal.shape
    columns = out_weight.shape[1] // 2
    whole, remote = pl.BlockSpec(memory_space=pltpu.VMEM), pl.BlockSpec(memory_space=pltpu.HBM)
    out_weight = pltpu.with_memory_space_constraint(out_weight, pltpu.HBM)

    def common(width):
        return {
            "scratch_shapes": [
                pltpu.VMEM((width // WIDTH, channels, WIDTH), jnp.bfloat16),
                pltpu.SemaphoreType.DMA((width // WIDTH,)),
            ],
            "compiler_params": pltpu.CompilerParams(vmem_limit_bytes=20 * 2**20),
            "cost_estimate": pl.CostEstimate(
                flops=2 * tokens * channels * width, bytes_accessed=2 * channels * width, transcendentals=0
            ),
        }

    half = jax.ShapeDtypeStruct((tokens, columns // 2), jnp.bfloat16)
    gated, far_one = pl.pallas_call(
        far_kernel,
        out_shape=(jax.ShapeDtypeStruct((tokens, channels), jnp.bfloat16), half),
        in_specs=[whole] * 3 + [remote],
        out_specs=(whole, whole),
        **common(columns // 2),
    )(convolved, gate_signal, direct, out_weight)
    swap = [(0, 1), (1, 0)]
    arrived_one = lax.ppermute(far_one, "tp", swap)
    far_two = pl.pallas_call(
        functools.partial(rest_kernel, True),
        out_shape=half,
        in_specs=[whole, remote],
        out_specs=whole,
        **common(columns // 2),
    )(gated, out_weight)
    arrived_two = lax.ppermute(far_two, "tp", swap)
    near = pl.pallas_call(
        functools.partial(rest_kernel, False),
        out_shape=jax.ShapeDtypeStruct((tokens, columns), jnp.float32),
        in_specs=[whole, remote],
        out_specs=whole,
        **common(columns),
    )(gated, out_weight)
    arrived = jnp.concatenate([arrived_one, arrived_two], axis=1).astype(jnp.float32)
    return (near + arrived).astype(jnp.bfloat16)


def butterfly(parts, sign):
    count = len(parts)
    if count == 1:
        return parts
    even, odd = butterfly(parts[0::2], sign), butterfly(parts[1::2], sign)
    half = count // 2
    low, high = [], []
    for j in range(half):
        real, imag = odd[j]
        if 4 * j == count:
            real, imag = (-imag, real) if sign > 0 else (imag, -real)
        elif j:
            c, s = math.cos(2.0 * math.pi * j / count), sign * math.sin(2.0 * math.pi * j / count)
            if 8 * j == count:
                real, imag = ((real - imag) * c, (real + imag) * c) if sign > 0 else ((real + imag) * c, (imag - real) * c)
            elif 8 * j == 3 * count:
                real, imag = ((real + imag) * c, (imag - real) * c) if sign > 0 else ((real - imag) * c, (real + imag) * c)
            else:
                real, imag = real * c - imag * s, real * s + imag * c
        low.append((even[j][0] + real, even[j][1] + imag))
        high.append((even[j][0] - real, even[j][1] - imag))
    return low + high


def turned(pair, cosine, sine):
    real, imag = pair
    return real * cosine - imag * sine, imag * cosine + real * sine


def scaled(pair, factor):
    return turned(pair, *factor)


def transform_kernel(
    taken_ref, *refs,
):
    tables, out_ref = refs[:6], refs[6]
    result_ref, packed, inner, flipped, high_ref, low_ref, done, sems = refs[7:15]
    held, table_sems = refs[15:21], refs[21]
    fwd_high, fwd_low, inv_high, inv_low, cos_ref, sin_ref = held
    loads = [pltpu.make_async_copy(*p, table_sems.at[i]) for i, p in enumerate(zip(tables, held))]
    for load in loads:
        load.start()
    devices, tokens, block = done.shape
    depth = packed.shape[0]
    half = cos_ref.shape[1]
    lane = [pl.ds(v * block, block) for v in range(RADIX)]
    spectrum_real, spectrum_imag = pl.ds(tokens, half), pl.ds(tokens + half, half)

    part = half // RADIX
    matrix = gather_rows(half, RADIX)
    for k in range(0, RADIX, 2):
        slabs = [taken_ref[2 * k + q, pl.ds(0, tokens), :] for q in range(4)]
        both = exact_rows(
            matrix, jnp.concatenate(slabs[:2], axis=0), jnp.concatenate(slabs[2:], axis=0)
        )
        for v in range(RADIX):
            rows = both[v * part : (v + 1) * part]
            packed[pl.ds(k * part, part), lane[v]] = rows[:, :block]
            packed[pl.ds((k + 1) * part, part), lane[v]] = rows[:, block:]

    wide = 2 * block
    loads[0].wait()
    loads[1].wait()
    for v in range(0, RADIX, 2):
        lanes = pl.ds(v * block, wide)
        right = packed[:, lanes]
        inner[:, lanes] = jnp.dot(fwd_high[...], right, preferred_element_type=jnp.float32) + jnp.dot(
            fwd_low[...], right, preferred_element_type=jnp.float32
        )

    row = lax.broadcasted_iota(jnp.int32, (half, half), 0)
    column = lax.broadcasted_iota(jnp.int32, (half, half), 1)
    flip = jnp.where(row + column == half, 1.0, 0.0).astype(jnp.bfloat16)
    for j in range(RADIX):
        source = 2 * RADIX - 1 - 2 * j
        right = jnp.concatenate(
            [taken_ref[source, spectrum_real, :], taken_ref[source, spectrum_imag, :]], axis=1
        )
        flipped[j] = jnp.dot(flip, right, preferred_element_type=jnp.float32).astype(jnp.bfloat16)

    def products(rows, start, parts):
        parts = butterfly(parts, -1)
        result = []
        for j in range(RADIX):
            real = taken_ref[2 * j, pl.ds(start + tokens, ROWS), :].astype(jnp.float32)
            imag = taken_ref[2 * j, pl.ds(start + tokens + half, ROWS), :].astype(jnp.float32)
            mirror = flipped[j, rows, :].astype(jnp.float32)
            result.append(scaled(parts[j], (real + mirror[:, :block], imag - mirror[:, block:])))
        return butterfly(result, 1)

    def middle(start, first):
        rows = pl.ds(start, ROWS)
        rows_imag = pl.ds(start + half, ROWS)
        top = lax.broadcasted_iota(jnp.int32, (ROWS, block), 0) == 0
        parts, tops = [], []
        for v in range(RADIX):
            real, imag = inner[rows, lane[v]], -inner[rows_imag, lane[v]]
            if first:
                tops.append(-imag)
                imag = jnp.where(top, 0.0, imag)
            if v:
                real, imag = turned((real, imag), cos_ref[v, rows, :], -sin_ref[v, rows, :])
            parts.append((real, imag))
        parts = products(rows, start, parts)
        if first:
            angles = [math.pi * v / RADIX for v in range(RADIX)]
            nyquist = [(t * math.cos(a), t * -math.sin(a)) for t, a in zip(tops, angles)]
            nyquist = butterfly(nyquist, -1)
            nyquist = [
                scaled(
                    nyquist[j],
                    (
                        taken_ref[2 * j + 1, pl.ds(tokens, ROWS), :].astype(jnp.float32),
                        taken_ref[2 * j + 1, pl.ds(tokens + half, ROWS), :].astype(jnp.float32),
                    ),
                )
                for j in range(RADIX)
            ]
            nyquist = butterfly(nyquist, 1)
            tops = [n[0] * math.cos(a) - n[1] * math.sin(a) for n, a in zip(nyquist, angles)]
        for v in range(RADIX):
            real, imag = parts[v]
            if v:
                real, imag = turned((real, imag), cos_ref[v, rows, :], sin_ref[v, rows, :])
            imag = jnp.where(top, tops[v], -imag) if first else -imag
            high_ref[rows, lane[v]], low_ref[rows, lane[v]] = split(real)
            high_ref[rows_imag, lane[v]], low_ref[rows_imag, lane[v]] = split(imag)

    for load in loads[2:]:
        load.wait()
    middle(0, True)

    @pl.loop(1, half // ROWS)
    def _(i):
        middle(pl.multiple_of(i * ROWS, ROWS), False)

    for v in range(0, RADIX, 2):
        lanes = pl.ds(v * block, wide)
        right = high_ref[:, lanes]
        result = (
            jnp.dot(inv_high[...], right, preferred_element_type=jnp.float32)
            + jnp.dot(inv_low[...], right, preferred_element_type=jnp.float32)
            + jnp.dot(inv_high[...], low_ref[:, lanes], preferred_element_type=jnp.float32)
        ) * (0.5 / (devices * tokens))
        result_ref[:, lanes] = result.astype(jnp.bfloat16)

    matrix = gather_rows(half, RADIX, invert=True)
    copies = []
    for k in range(0, RADIX, 2):
        slabs = [
            jnp.concatenate([result_ref[pl.ds(p * part, part), lane[v]] for v in range(RADIX)], axis=0)
            for p in (k, k + 1)
        ]
        both = exact_rows(matrix, *slabs)
        for q in range(4):
            done[2 * k + q] = both[(q % 2) * tokens : (q % 2 + 1) * tokens, (q // 2) * block : (q // 2 + 1) * block]
        copies.append(
            pltpu.make_async_copy(
                done.at[pl.ds(2 * k, 4)], out_ref.at[pl.ds(2 * k, 4)], sems.at[k // 2]
            )
        )
        copies[-1].start()
    for copy in copies:
        copy.wait()


def angles_of(shape, rows, columns, order):
    index = lax.broadcasted_iota(jnp.int32, shape, rows) * lax.broadcasted_iota(jnp.int32, shape, columns)
    return (2.0 * math.pi / order) * (index & (order - 1)).astype(jnp.float32)


def tables_kernel(fwd_high, fwd_low, inv_high, inv_low, cos_ref, sin_ref):
    depth = fwd_high.shape[1]
    _, half, block = cos_ref.shape
    order = 2 * RADIX * half

    def alternating(shape, dim):
        return (1 - 2 * (lax.broadcasted_iota(jnp.int32, shape, dim) & 1)).astype(jnp.float32)

    def first(shape, dim):
        return lax.broadcasted_iota(jnp.int32, shape, dim) == 0

    shape = (half, depth)
    angle = angles_of(shape, 0, 1, 2 * half)
    fwd_high[:half], fwd_low[:half] = split(jnp.cos(angle))
    sine = jnp.where(first(shape, 0), alternating(shape, 1), jnp.sin(angle))
    fwd_high[half:], fwd_low[half:] = split(sine)
    shape = (depth, half)
    angle = angles_of(shape, 0, 1, 2 * half)
    inv_high[:, :half], inv_low[:, :half] = split(jnp.cos(angle))
    sine = jnp.where(first(shape, 1), alternating(shape, 0), jnp.sin(angle))
    inv_high[:, half:], inv_low[:, half:] = split(sine)

    for v in range(RADIX):
        step = lax.broadcasted_iota(jnp.int32, (half, block), 0).astype(jnp.float32)
        angle = (2.0 * math.pi * v / order) * step
        cos_ref[v] = jnp.cos(angle)
        sin_ref[v] = jnp.sin(angle)


def local_tables(length, block):
    half, depth = length // RADIX, length // RADIX
    whole = pl.BlockSpec(memory_space=pltpu.VMEM)
    forward = jax.ShapeDtypeStruct((2 * half, depth), jnp.bfloat16)
    inverse = jax.ShapeDtypeStruct((depth, 2 * half), jnp.bfloat16)
    twiddle = jax.ShapeDtypeStruct((RADIX, half, block), jnp.float32)
    return pl.pallas_call(
        tables_kernel,
        out_shape=(forward, forward, inverse, inverse, twiddle, twiddle),
        out_specs=(whole,) * 6,
        compiler_params=pltpu.CompilerParams(vmem_limit_bytes=16 * 2**20),
        cost_estimate=pl.CostEstimate(
            flops=200 * RADIX * half * block, bytes_accessed=8 * RADIX * half * block, transcendentals=0
        ),
    )()


def local_transform(taken, tables, tokens):
    devices, _, block = taken.shape
    length = devices * tokens
    half, depth = length // RADIX, length // RADIX
    flops = 5 * 2 * 2 * half * depth * RADIX * block
    whole, remote = pl.BlockSpec(memory_space=pltpu.VMEM), pl.BlockSpec(memory_space=pltpu.HBM)
    wide = RADIX * block
    tables = [pltpu.with_memory_space_constraint(t, pltpu.HBM) for t in tables]
    return pl.pallas_call(
        transform_kernel,
        out_shape=pltpu.HBM((devices, tokens, block), jnp.bfloat16),
        in_specs=[whole] + [remote] * 6,
        out_specs=remote,
        scratch_shapes=[
            pltpu.VMEM((depth, wide), jnp.bfloat16),
            pltpu.VMEM((depth, wide), jnp.bfloat16),
            pltpu.VMEM((2 * half, wide), jnp.float32),
            pltpu.VMEM((RADIX, half, 2 * block), jnp.bfloat16),
            pltpu.VMEM((2 * half, wide), jnp.bfloat16),
            pltpu.VMEM((2 * half, wide), jnp.bfloat16),
            pltpu.VMEM((devices, tokens, block), jnp.bfloat16),
            pltpu.SemaphoreType.DMA((RADIX // 2,)),
            *(pltpu.VMEM(t.shape, t.dtype) for t in tables),
            pltpu.SemaphoreType.DMA((len(tables),)),
        ],
        compiler_params=pltpu.CompilerParams(vmem_limit_bytes=20 * 2**20),
        cost_estimate=pl.CostEstimate(flops=flops, bytes_accessed=taken.size * 2, transcendentals=0),
    )(taken, *tables)


def sum_shares(share, axis):
    count = lax.axis_size(axis)
    rank = lax.axis_index(axis)
    columns = share.shape[1] // count
    total = lax.dynamic_slice_in_dim(share, rank * columns, columns, axis=1)
    for step in range(1, count):
        piece = lax.dynamic_slice_in_dim(share, (rank + step) % count * columns, columns, axis=1)
        pairs = [(i, (i + step) % count) for i in range(count)]
        total = total + lax.ppermute(piece.astype(jnp.bfloat16), axis, pairs).astype(jnp.float32)
    return total


def fused_shards(query, key_in, value, short_taps, skip_gain, filter_spectrum, out_weight):
    devices = lax.axis_size("ctx")
    tokens, channels = query.shape
    tails = shifted_in(own_tails(query, key_in, value), "ctx")
    sent = packed_spectrum(filter_spectrum, devices)
    sent = with_signal(key_in, value, tails, short_taps, sent)
    taken = lax.all_to_all(sent, "ctx", split_axis=0, concat_axis=0, tiled=True)
    gate_signal, direct = gates(query, key_in, value, tails, short_taps, skip_gain)
    tables = local_tables(tokens * devices, channels // devices)
    convolved = local_transform(taken, tables, tokens)
    convolved = lax.all_to_all(convolved, "ctx", split_axis=0, concat_axis=0, tiled=True)
    return projected(convolved, gate_signal, direct, out_weight)


def shards(query, key_in, value, short_taps, skip_gain, filter_spectrum, out_weight):
    devices = lax.axis_size("ctx")
    tokens, channels = query.shape
    length, block = tokens * devices, channels // devices
    if block == LANES and devices == 2 * RADIX and lax.axis_size("tp") == 2:
        return fused_shards(query, key_in, value, short_taps, skip_gain, filter_spectrum, out_weight)
    tails = shifted_in(jnp.concatenate([query[-2:], key_in[-2:], value[-2:]], axis=0), "ctx")
    gate_signal = causal_filter(query, tails[0:2], short_taps[0])
    mixed_in = causal_filter(key_in, tails[2:4], short_taps[1]) * causal_filter(
        value, tails[4:6], short_taps[2]
    )
    own_signal = mixed_in.astype(jnp.bfloat16).reshape(tokens, devices, block).transpose(1, 0, 2)
    own_spectrum = (
        filter_spectrum.astype(jnp.bfloat16)
        .reshape(tokens, 2, 2, devices, block)
        .transpose(3, 2, 0, 1, 4)
        .reshape(devices, 4 * tokens, block)
    )
    sent = jnp.concatenate([own_signal, own_spectrum], axis=1)
    taken = lax.all_to_all(sent, "ctx", split_axis=0, concat_axis=0, tiled=True)
    signal = taken[:, :tokens].reshape(length, block)
    spectrum_real = taken[:, tokens : 3 * tokens].reshape(2 * length, block)
    spectrum_imag = taken[:, 3 * tokens :].reshape(2 * length, block)
    convolved = long_filter(signal, spectrum_real, spectrum_imag).astype(jnp.bfloat16)
    convolved = lax.all_to_all(
        convolved.reshape(devices, tokens, block), "ctx", split_axis=0, concat_axis=0, tiled=True
    )
    convolved = convolved.transpose(1, 0, 2).reshape(tokens, channels).astype(jnp.float32)
    gated = (gate_signal * (convolved + skip_gain * mixed_in)).astype(jnp.bfloat16)
    share = jnp.dot(gated, out_weight, preferred_element_type=jnp.float32)
    return sum_shares(share, "tp").astype(jnp.bfloat16)


def solution(mesh):
    return jax.shard_map(
        shards,
        mesh=mesh,
        in_specs=(
            P("ctx", "tp"),
            P("ctx", "tp"),
            P("ctx", "tp"),
            P(None, None, "tp"),
            P("tp"),
            P("ctx", None, None, "tp"),
            P("tp", None),
        ),
        out_specs=P("ctx", "tp"),
        check_vma=False,
    )
```

```python
import functools
import math

import jax
import jax.numpy as jnp
from jax import lax
from jax.experimental import pallas as pl
from jax.experimental.pallas import tpu as pltpu
from jax.sharding import PartitionSpec as P


RADIX = 8
ROWS = 16
LANES = 128
FAR_CHUNKS = (512, 512, 1024)
NEAR_WIDTH = 512
GROUP = 64
EDGE = 8


def shifted_in(rows, axis):
    count = lax.axis_size(axis)
    return lax.ppermute(rows, axis, [(i, i + 1) for i in range(count - 1)])


def causal_filter(signal, tail, taps):
    values = jnp.concatenate([tail, signal], axis=0).astype(jnp.float32)
    return taps[0] * values[2:] + taps[1] * values[1:-1] + taps[2] * values[:-2]


def turn(rows, columns, order):
    index = rows[:, None] * columns[None, :] % order
    angle = (2.0 * math.pi / order) * index.astype(jnp.float32)
    return jnp.cos(angle), jnp.sin(angle)


def exact_dot(left, right):
    return jnp.dot(left, right, precision=lax.Precision.HIGHEST, preferred_element_type=jnp.float32)


def radix_of(order):
    return 2 ** ((order.bit_length() - 1) // 2)


def long_filter(signal, spectrum_real, spectrum_imag):
    length, width = signal.shape
    order = spectrum_real.shape[0]
    radix = radix_of(order)
    span, depth = order // radix, length // radix
    low = jnp.arange(span, dtype=jnp.int32)
    deep = jnp.arange(depth, dtype=jnp.int32)
    lanes = jnp.arange(radix, dtype=jnp.int32)
    inner_cos, inner_sin = turn(low, deep, span)
    twiddle_cos, twiddle_sin = (t[:, :, None] for t in turn(lanes, low, order))
    outer_cos, outer_sin = turn(lanes, lanes, radix)

    samples = signal.astype(jnp.float32).reshape(depth, radix * width)
    real = exact_dot(inner_cos, samples).reshape(span, radix, width).transpose(1, 0, 2)
    imag = -exact_dot(inner_sin, samples).reshape(span, radix, width).transpose(1, 0, 2)
    real, imag = (
        (real * twiddle_cos + imag * twiddle_sin).reshape(radix, span * width),
        (imag * twiddle_cos - real * twiddle_sin).reshape(radix, span * width),
    )
    real, imag = (
        exact_dot(outer_cos, real) + exact_dot(outer_sin, imag),
        exact_dot(outer_cos, imag) - exact_dot(outer_sin, real),
    )
    spectrum_real = spectrum_real.astype(jnp.float32).reshape(radix, span * width)
    spectrum_imag = spectrum_imag.astype(jnp.float32).reshape(radix, span * width)
    real, imag = (
        real * spectrum_real - imag * spectrum_imag,
        real * spectrum_imag + imag * spectrum_real,
    )
    real, imag = (
        (exact_dot(outer_cos, real) - exact_dot(outer_sin, imag)).reshape(radix, span, width),
        (exact_dot(outer_cos, imag) + exact_dot(outer_sin, real)).reshape(radix, span, width),
    )
    real, imag = (
        (real * twiddle_cos - imag * twiddle_sin).transpose(1, 0, 2).reshape(span, radix * width),
        (imag * twiddle_cos + real * twiddle_sin).transpose(1, 0, 2).reshape(span, radix * width),
    )
    result = exact_dot(inner_cos.T, real) - exact_dot(inner_sin.T, imag)
    return (result / order).reshape(length, width)


def split(value):
    high = value.astype(jnp.bfloat16)
    return high, (value - high.astype(jnp.float32)).astype(jnp.bfloat16)


def filtered_block(signal_ref, tails_ref, taps_ref, which, lanes):
    values = signal_ref[:, lanes].astype(jnp.float32)
    tails = tails_ref[:, lanes].astype(jnp.float32)
    older, newer = tails[2 * which : 2 * which + 1], tails[2 * which + 1 : 2 * which + 2]
    row = lax.broadcasted_iota(jnp.int32, values.shape, 0)
    one_back = jnp.where(row == 0, newer, pltpu.roll(values, 1, 0))
    two_back = jnp.where(row == 0, older, jnp.where(row == 1, newer, pltpu.roll(values, 2, 0)))
    taps = taps_ref[which, :, lanes]
    return taps[0:1] * values + taps[1:2] * one_back + taps[2:3] * two_back


def tails_kernel(query_ref, key_ref, value_ref, tails_ref):
    rows = query_ref.shape[0]
    for which, ref in enumerate((query_ref, key_ref, value_ref)):
        tails_ref[2 * which : 2 * which + 2, :] = ref[...].astype(jnp.float32)[rows - 2 :].astype(jnp.bfloat16)


def own_tails(query, key_in, value):
    tokens, channels = query.shape
    last = pl.BlockSpec((ROWS, channels), lambda i: (tokens // ROWS - 1, 0))
    return pl.pallas_call(
        tails_kernel,
        grid=(1,),
        out_shape=jax.ShapeDtypeStruct((6, channels), query.dtype),
        in_specs=[last] * 3,
        out_specs=pl.BlockSpec((6, channels), lambda i: (0, 0)),
        compiler_params=pltpu.CompilerParams(vmem_limit_bytes=4 * 2**20),
    )(*(pltpu.with_memory_space_constraint(a, pltpu.HBM) for a in (query, key_in, value)))


def gather_rows(size, count, invert=False):
    row = lax.broadcasted_iota(jnp.int32, (size, size), 0)
    column = lax.broadcasted_iota(jnp.int32, (size, size), 1)
    if invert:
        row, column = column, row
    inner = size // count
    match = column == (row % inner) * count + row // inner
    return jnp.where(match, 1.0, 0.0).astype(jnp.bfloat16)


def exact_rows(matrix, left, right):
    both = jnp.concatenate([left, right], axis=1)
    return jnp.dot(matrix, both, preferred_element_type=jnp.float32).astype(jnp.bfloat16)


def unshifted(values, taps):
    return taps[0:1] * values + taps[1:2] * pltpu.roll(values, 1, 0) + taps[2:3] * pltpu.roll(values, 2, 0)


def prepare_kernel(spectrum_ref, key_ref, value_ref, taps_ref, sent_ref, *scratch):
    spectrum, key, value, taps, staged, in_sems, out_sems = scratch
    devices, _, block = staged.shape
    tokens = key.shape[0]
    fine = 2 * devices
    slab = GROUP * fine
    groups = spectrum.shape[0] // slab
    loads = [
        pltpu.make_async_copy(source, target, in_sems.at[i])
        for i, (source, target) in enumerate(((taps_ref, taps), (key_ref, key), (value_ref, value)))
    ] + [
        pltpu.make_async_copy(
            spectrum_ref.at[pl.ds(g * slab, slab)], spectrum.at[pl.ds(g * slab, slab)], in_sems.at[3 + g]
        )
        for g in range(groups)
    ]
    for load in loads:
        load.start()
    stores = []

    def store(start, size):
        rows = pl.ds(start, size)
        stores.append(
            pltpu.make_async_copy(staged.at[:, rows], sent_ref.at[:, rows], out_sems.at[len(stores)])
        )
        stores[-1].start()

    for load in loads[:3]:
        load.wait()
    edge = tokens + 2 * GROUP * groups
    for j in range(devices):
        lanes = pl.ds(j * block, block)
        k, v = key[:, lanes].astype(jnp.float32), value[:, lanes].astype(jnp.float32)
        mixed = unshifted(k, taps[1, :, lanes]) * unshifted(v, taps[2, :, lanes])
        staged[j, pl.ds(0, tokens), :] = mixed.astype(jnp.bfloat16)
        ends = jnp.concatenate([k[:2], v[:2], k[tokens - 2 :], v[tokens - 2 :]], axis=0)
        staged[j, pl.ds(edge, EDGE), :] = ends.astype(jnp.bfloat16)
    store(0, tokens)
    store(edge, EDGE)

    for g in range(groups):
        loads[3 + g].wait()
        start = tokens + 2 * GROUP * g
        for s in range(fine):
            staged[s // 2, pl.ds(start + s % 2 * GROUP, GROUP), :] = spectrum[
                pl.ds(g * GROUP * fine + s, GROUP, stride=fine), :
            ].astype(jnp.bfloat16)
        store(start, 2 * GROUP)
    for copy in stores:
        copy.wait()


def prepared(key_in, value, short_taps, filter_spectrum, devices):
    tokens, _, _, channels = filter_spectrum.shape
    block, pairs = channels // devices, 2 * tokens
    groups = pairs // GROUP
    view = (
        filter_spectrum.reshape(tokens, 2, 2, devices, block)
        .transpose(0, 1, 3, 2, 4)
        .reshape(2 * pairs * devices, block)
    )
    rows = tokens + 2 * pairs + EDGE
    remote = pl.BlockSpec(memory_space=pltpu.HBM)
    inputs = [
        pltpu.with_memory_space_constraint(a, pltpu.HBM) for a in (view, key_in, value, short_taps)
    ]
    return pl.pallas_call(
        prepare_kernel,
        out_shape=pltpu.HBM((devices, rows, block), jnp.bfloat16),
        in_specs=[remote] * 4,
        out_specs=remote,
        scratch_shapes=[
            pltpu.VMEM(view.shape, jnp.float32),
            pltpu.VMEM((tokens, channels), jnp.bfloat16),
            pltpu.VMEM((tokens, channels), jnp.bfloat16),
            pltpu.VMEM(short_taps.shape, jnp.float32),
            pltpu.VMEM((devices, rows, block), jnp.bfloat16),
            pltpu.SemaphoreType.DMA((3 + groups,)),
            pltpu.SemaphoreType.DMA((2 + groups,)),
        ],
        compiler_params=pltpu.CompilerParams(vmem_limit_bytes=20 * 2**20),
        cost_estimate=pl.CostEstimate(flops=0, bytes_accessed=view.size * 6, transcendentals=0),
    )(*inputs)


def gate_kernel(query_ref, key_ref, value_ref, tails_ref, taps_ref, gain_ref, gate_ref, direct_ref):
    _, channels = query_ref.shape
    for j in range(channels // LANES):
        lanes = pl.ds(j * LANES, LANES)
        mixed = filtered_block(key_ref, tails_ref, taps_ref, 1, lanes) * filtered_block(
            value_ref, tails_ref, taps_ref, 2, lanes
        )
        gate_ref[:, lanes] = filtered_block(query_ref, tails_ref, taps_ref, 0, lanes)
        direct_ref[:, lanes] = gain_ref[:, lanes] * mixed


def gates(query, key_in, value, tails, short_taps, skip_gain):
    shape = jax.ShapeDtypeStruct(query.shape, jnp.float32)
    whole = pl.BlockSpec(memory_space=pltpu.VMEM)
    return pl.pallas_call(
        gate_kernel,
        out_shape=(shape, shape),
        in_specs=[whole] * 6,
        out_specs=(whole, whole),
        compiler_params=pltpu.CompilerParams(vmem_limit_bytes=16 * 2**20),
        cost_estimate=pl.CostEstimate(
            flops=20 * query.size, bytes_accessed=14 * query.size, transcendentals=0
        ),
    )(query, key_in, value, tails, short_taps, skip_gain[None, :])


def column_copies(weight_ref, held, sems, first):
    chunks, _, width = held.shape
    return [
        pltpu.make_async_copy(
            weight_ref.at[:, pl.ds(pl.multiple_of(first + i * width, LANES), width)],
            held.at[i],
            sems.at[i],
        )
        for i in range(chunks)
    ]


def multiply(gated_ref, share_ref, held, copies):
    width = held.shape[2]
    for i, copy in enumerate(copies):
        copy.wait()
        share_ref[:, pl.ds(i * width, width)] = jnp.dot(
            gated_ref[...], held[i], preferred_element_type=jnp.float32
        ).astype(share_ref.dtype)


def gated_kernel(conv_ref, gate_ref, direct_ref, weight_ref, gated_ref, share_ref, held, sems):
    devices, _, block = conv_ref.shape
    columns = weight_ref.shape[1] // 2
    copies = column_copies(weight_ref, held, sems, (1 - lax.axis_index("tp")) * columns)
    for copy in copies:
        copy.start()
    for j in range(devices):
        lanes = pl.ds(j * block, block)
        gated_ref[:, lanes] = (
            gate_ref[:, lanes] * (conv_ref[j].astype(jnp.float32) + direct_ref[:, lanes])
        ).astype(jnp.bfloat16)
    multiply(gated_ref, share_ref, held, copies)


def share_kernel(far, offset, gated_ref, weight_ref, share_ref, held, sems):
    columns = weight_ref.shape[1] // 2
    rank = lax.axis_index("tp")
    copies = column_copies(weight_ref, held, sems, (1 - rank if far else rank) * columns + offset)
    for copy in copies:
        copy.start()
    multiply(gated_ref, share_ref, held, copies)


def projected(convolved, gate_signal, direct, out_weight):
    tokens, channels = gate_signal.shape
    columns = out_weight.shape[1] // 2
    whole, remote = pl.BlockSpec(memory_space=pltpu.VMEM), pl.BlockSpec(memory_space=pltpu.HBM)
    out_weight = pltpu.with_memory_space_constraint(out_weight, pltpu.HBM)

    def share(kernel, operands, extra, width, step, dtype):
        return pl.pallas_call(
            kernel,
            out_shape=(*extra, jax.ShapeDtypeStruct((tokens, width), dtype)),
            in_specs=[whole] * len(operands) + [remote],
            out_specs=(whole,) * (len(extra) + 1),
            scratch_shapes=[
                pltpu.VMEM((width // step, channels, step), jnp.bfloat16),
                pltpu.SemaphoreType.DMA((width // step,)),
            ],
            compiler_params=pltpu.CompilerParams(vmem_limit_bytes=20 * 2**20),
            cost_estimate=pl.CostEstimate(
                flops=2 * tokens * channels * width, bytes_accessed=2 * channels * width, transcendentals=0
            ),
        )(*operands, out_weight)

    swap = [(0, 1), (1, 0)]
    widths = FAR_CHUNKS if sum(FAR_CHUNKS) == columns else (columns,)
    arrived, offset, gated = [], 0, None
    for width in widths:
        if gated is None:
            gated, far = share(
                gated_kernel,
                (convolved, gate_signal, direct),
                (jax.ShapeDtypeStruct((tokens, channels), jnp.bfloat16),),
                width,
                min(width, NEAR_WIDTH),
                jnp.bfloat16,
            )
        else:
            kernel = functools.partial(share_kernel, True, offset)
            (far,) = share(kernel, (gated,), (), width, min(width, NEAR_WIDTH), jnp.bfloat16)
        arrived.append(lax.ppermute(far, "tp", swap))
        offset += width
    kernel = functools.partial(share_kernel, False, 0)
    (near,) = share(kernel, (gated,), (), columns, NEAR_WIDTH, jnp.float32)
    return (near + jnp.concatenate(arrived, axis=1).astype(jnp.float32)).astype(jnp.bfloat16)


def butterfly(parts, sign):
    count = len(parts)
    if count == 1:
        return parts
    even, odd = butterfly(parts[0::2], sign), butterfly(parts[1::2], sign)
    half = count // 2
    low, high = [], []
    for j in range(half):
        real, imag = odd[j]
        if 4 * j == count:
            real, imag = (-imag, real) if sign > 0 else (imag, -real)
        elif j:
            c, s = math.cos(2.0 * math.pi * j / count), sign * math.sin(2.0 * math.pi * j / count)
            if 8 * j == count:
                real, imag = ((real - imag) * c, (real + imag) * c) if sign > 0 else ((real + imag) * c, (imag - real) * c)
            elif 8 * j == 3 * count:
                real, imag = ((real + imag) * c, (imag - real) * c) if sign > 0 else ((real - imag) * c, (real + imag) * c)
            else:
                real, imag = real * c - imag * s, real * s + imag * c
        low.append((even[j][0] + real, even[j][1] + imag))
        high.append((even[j][0] - real, even[j][1] - imag))
    return low + high


def turned(pair, cosine, sine):
    real, imag = pair
    return real * cosine - imag * sine, imag * cosine + real * sine


def scaled(pair, factor):
    return turned(pair, *factor)


def transform_kernel(
    taken_ref, taps_ref, *refs,
):
    tables, out_ref = refs[:6], refs[6]
    result_ref, packed, inner, flipped, high_ref, low_ref, done, sems = refs[7:15]
    held, table_sems, edges = refs[15:21], refs[21], refs[22]
    fwd_high, fwd_low, inv_high, inv_low, cos_ref, sin_ref = held
    loads = [pltpu.make_async_copy(*p, table_sems.at[i]) for i, p in enumerate(zip(tables, held))]
    for load in loads:
        load.start()
    devices, tokens, block = done.shape
    half = cos_ref.shape[1]
    lane = [pl.ds(v * block, block) for v in range(RADIX)]
    edge = tokens + 2 * half

    edges[:EDGE] = jnp.zeros((EDGE, block), jnp.float32)
    for q in range(devices):
        edges[pl.ds((q + 1) * EDGE, EDGE)] = taken_ref[q, pl.ds(edge, EDGE), :].astype(jnp.float32)

    def ends(index, own):
        return edges[pl.ds(index + EDGE * own, devices, stride=EDGE), :]

    def first_rows(which):
        taps = taps_ref[which]
        base = 2 * (which - 1)
        now, after = ends(base, 1), ends(base + 1, 1)
        older, newer = ends(base + 4, 0), ends(base + 5, 0)
        return (
            taps[0:1] * now + taps[1:2] * newer + taps[2:3] * older,
            taps[0:1] * after + taps[1:2] * now + taps[2:3] * newer,
        )

    key_rows, value_rows = first_rows(1), first_rows(2)
    first_row, second_row = key_rows[0] * value_rows[0], key_rows[1] * value_rows[1]

    def tokens_of(q):
        top = taken_ref[q, pl.ds(0, ROWS), :].astype(jnp.float32)
        index = lax.broadcasted_iota(jnp.int32, top.shape, 0)
        top = jnp.where(index == 0, first_row[q : q + 1], jnp.where(index == 1, second_row[q : q + 1], top))
        return jnp.concatenate(
            [top.astype(jnp.bfloat16), taken_ref[q, pl.ds(ROWS, tokens - ROWS), :]], axis=0
        )

    def spectrum_rows(start, imag):
        return pl.ds(tokens + start // GROUP * 2 * GROUP + start % GROUP + imag * GROUP, ROWS)

    part = half // RADIX
    matrix = gather_rows(half, RADIX)
    for k in range(0, RADIX, 2):
        slabs = [tokens_of(2 * k + q) for q in range(4)]
        both = exact_rows(
            matrix, jnp.concatenate(slabs[:2], axis=0), jnp.concatenate(slabs[2:], axis=0)
        )
        for v in range(RADIX):
            rows = both[v * part : (v + 1) * part]
            packed[pl.ds(k * part, part), lane[v]] = rows[:, :block]
            packed[pl.ds((k + 1) * part, part), lane[v]] = rows[:, block:]

    row = lax.broadcasted_iota(jnp.int32, (half, half), 0)
    column = lax.broadcasted_iota(jnp.int32, (half, half), 1)
    flip = jnp.where(row + column == half, 1.0, 0.0).astype(jnp.bfloat16)
    for j in range(RADIX):
        source = 2 * RADIX - 1 - 2 * j
        right = jnp.concatenate(
            [
                jnp.concatenate(
                    [
                        taken_ref[source, pl.ds(tokens + (2 * g + imag) * GROUP, GROUP), :]
                        for g in range(half // GROUP)
                    ],
                    axis=0,
                )
                for imag in range(2)
            ],
            axis=1,
        )
        flipped[j] = jnp.dot(flip, right, preferred_element_type=jnp.float32).astype(jnp.bfloat16)

    wide = 2 * block
    loads[0].wait()
    loads[1].wait()
    for v in range(0, RADIX, 2):
        lanes = pl.ds(v * block, wide)
        right = packed[:, lanes]
        inner[:, lanes] = jnp.dot(fwd_high[...], right, preferred_element_type=jnp.float32) + jnp.dot(
            fwd_low[...], right, preferred_element_type=jnp.float32
        )

    def products(rows, start, parts):
        parts = butterfly(parts, -1)
        result = []
        for j in range(RADIX):
            real = taken_ref[2 * j, spectrum_rows(start, 0), :].astype(jnp.float32)
            imag = taken_ref[2 * j, spectrum_rows(start, 1), :].astype(jnp.float32)
            mirror = flipped[j, rows, :].astype(jnp.float32)
            result.append(scaled(parts[j], (real + mirror[:, :block], imag - mirror[:, block:])))
        return butterfly(result, 1)

    def middle(start, first):
        rows = pl.ds(start, ROWS)
        rows_imag = pl.ds(start + half, ROWS)
        top = lax.broadcasted_iota(jnp.int32, (ROWS, block), 0) == 0
        parts, tops = [], []
        for v in range(RADIX):
            real, imag = inner[rows, lane[v]], -inner[rows_imag, lane[v]]
            if first:
                tops.append(-imag)
                imag = jnp.where(top, 0.0, imag)
            if v:
                real, imag = turned((real, imag), cos_ref[v, rows, :], -sin_ref[v, rows, :])
            parts.append((real, imag))
        parts = products(rows, start, parts)
        if first:
            angles = [math.pi * v / RADIX for v in range(RADIX)]
            nyquist = [(t * math.cos(a), t * -math.sin(a)) for t, a in zip(tops, angles)]
            nyquist = butterfly(nyquist, -1)
            nyquist = [
                scaled(
                    nyquist[j],
                    (
                        taken_ref[2 * j + 1, spectrum_rows(0, 0), :].astype(jnp.float32),
                        taken_ref[2 * j + 1, spectrum_rows(0, 1), :].astype(jnp.float32),
                    ),
                )
                for j in range(RADIX)
            ]
            nyquist = butterfly(nyquist, 1)
            tops = [n[0] * math.cos(a) - n[1] * math.sin(a) for n, a in zip(nyquist, angles)]
        for v in range(RADIX):
            real, imag = parts[v]
            if v:
                real, imag = turned((real, imag), cos_ref[v, rows, :], sin_ref[v, rows, :])
            imag = jnp.where(top, tops[v], -imag) if first else -imag
            high_ref[rows, lane[v]], low_ref[rows, lane[v]] = split(real)
            high_ref[rows_imag, lane[v]], low_ref[rows_imag, lane[v]] = split(imag)

    for load in loads[2:]:
        load.wait()
    middle(0, True)

    @pl.loop(1, half // ROWS)
    def _(i):
        middle(pl.multiple_of(i * ROWS, ROWS), False)

    for v in range(0, RADIX, 2):
        lanes = pl.ds(v * block, wide)
        right = high_ref[:, lanes]
        result = (
            jnp.dot(inv_high[...], right, preferred_element_type=jnp.float32)
            + jnp.dot(inv_low[...], right, preferred_element_type=jnp.float32)
            + jnp.dot(inv_high[...], low_ref[:, lanes], preferred_element_type=jnp.float32)
        ) * (0.5 / (devices * tokens))
        result_ref[:, lanes] = result.astype(jnp.bfloat16)

    matrix = gather_rows(half, RADIX, invert=True)
    copies = []
    for k in range(0, RADIX, 2):
        slabs = [
            jnp.concatenate([result_ref[pl.ds(p * part, part), lane[v]] for v in range(RADIX)], axis=0)
            for p in (k, k + 1)
        ]
        both = exact_rows(matrix, *slabs)
        for q in range(4):
            done[2 * k + q] = both[(q % 2) * tokens : (q % 2 + 1) * tokens, (q // 2) * block : (q // 2 + 1) * block]
        copies.append(
            pltpu.make_async_copy(
                done.at[pl.ds(2 * k, 4)], out_ref.at[pl.ds(2 * k, 4)], sems.at[k // 2]
            )
        )
        copies[-1].start()
    for copy in copies:
        copy.wait()


def angles_of(shape, rows, columns, order):
    index = lax.broadcasted_iota(jnp.int32, shape, rows) * lax.broadcasted_iota(jnp.int32, shape, columns)
    return (2.0 * math.pi / order) * (index & (order - 1)).astype(jnp.float32)


def tables_kernel(fwd_high, fwd_low, inv_high, inv_low, cos_ref, sin_ref):
    depth = fwd_high.shape[1]
    _, half, block = cos_ref.shape
    order = 2 * RADIX * half

    def alternating(shape, dim):
        return (1 - 2 * (lax.broadcasted_iota(jnp.int32, shape, dim) & 1)).astype(jnp.float32)

    def first(shape, dim):
        return lax.broadcasted_iota(jnp.int32, shape, dim) == 0

    shape = (half, depth)
    angle = angles_of(shape, 0, 1, 2 * half)
    fwd_high[:half], fwd_low[:half] = split(jnp.cos(angle))
    sine = jnp.where(first(shape, 0), alternating(shape, 1), jnp.sin(angle))
    fwd_high[half:], fwd_low[half:] = split(sine)
    shape = (depth, half)
    angle = angles_of(shape, 0, 1, 2 * half)
    inv_high[:, :half], inv_low[:, :half] = split(jnp.cos(angle))
    sine = jnp.where(first(shape, 1), alternating(shape, 0), jnp.sin(angle))
    inv_high[:, half:], inv_low[:, half:] = split(sine)

    for v in range(RADIX):
        step = lax.broadcasted_iota(jnp.int32, (half, block), 0).astype(jnp.float32)
        angle = (2.0 * math.pi * v / order) * step
        cos_ref[v] = jnp.cos(angle)
        sin_ref[v] = jnp.sin(angle)


def local_tables(length, block):
    half, depth = length // RADIX, length // RADIX
    whole = pl.BlockSpec(memory_space=pltpu.VMEM)
    forward = jax.ShapeDtypeStruct((2 * half, depth), jnp.bfloat16)
    inverse = jax.ShapeDtypeStruct((depth, 2 * half), jnp.bfloat16)
    twiddle = jax.ShapeDtypeStruct((RADIX, half, block), jnp.float32)
    return pl.pallas_call(
        tables_kernel,
        out_shape=(forward, forward, inverse, inverse, twiddle, twiddle),
        out_specs=(whole,) * 6,
        compiler_params=pltpu.CompilerParams(vmem_limit_bytes=16 * 2**20),
        cost_estimate=pl.CostEstimate(
            flops=200 * RADIX * half * block, bytes_accessed=8 * RADIX * half * block, transcendentals=0
        ),
    )()


def local_transform(taken, taps, tables, tokens):
    devices, _, block = taken.shape
    length = devices * tokens
    half, depth = length // RADIX, length // RADIX
    flops = 5 * 2 * 2 * half * depth * RADIX * block
    whole, remote = pl.BlockSpec(memory_space=pltpu.VMEM), pl.BlockSpec(memory_space=pltpu.HBM)
    wide = RADIX * block
    tables = [pltpu.with_memory_space_constraint(t, pltpu.HBM) for t in tables]
    return pl.pallas_call(
        transform_kernel,
        out_shape=pltpu.HBM((devices, tokens, block), jnp.bfloat16),
        in_specs=[whole] * 2 + [remote] * 6,
        out_specs=remote,
        scratch_shapes=[
            pltpu.VMEM((depth, wide), jnp.bfloat16),
            pltpu.VMEM((depth, wide), jnp.bfloat16),
            pltpu.VMEM((2 * half, wide), jnp.float32),
            pltpu.VMEM((RADIX, half, 2 * block), jnp.bfloat16),
            pltpu.VMEM((2 * half, wide), jnp.bfloat16),
            pltpu.VMEM((2 * half, wide), jnp.bfloat16),
            pltpu.VMEM((devices, tokens, block), jnp.bfloat16),
            pltpu.SemaphoreType.DMA((RADIX // 2,)),
            *(pltpu.VMEM(t.shape, t.dtype) for t in tables),
            pltpu.SemaphoreType.DMA((len(tables),)),
            pltpu.VMEM(((devices + 1) * EDGE, block), jnp.float32),
        ],
        compiler_params=pltpu.CompilerParams(vmem_limit_bytes=20 * 2**20),
        cost_estimate=pl.CostEstimate(flops=flops, bytes_accessed=taken.size * 2, transcendentals=0),
    )(taken, taps, *tables)


def sum_shares(share, axis):
    count = lax.axis_size(axis)
    rank = lax.axis_index(axis)
    columns = share.shape[1] // count
    total = lax.dynamic_slice_in_dim(share, rank * columns, columns, axis=1)
    for step in range(1, count):
        piece = lax.dynamic_slice_in_dim(share, (rank + step) % count * columns, columns, axis=1)
        pairs = [(i, (i + step) % count) for i in range(count)]
        total = total + lax.ppermute(piece.astype(jnp.bfloat16), axis, pairs).astype(jnp.float32)
    return total


def fused_shards(query, key_in, value, short_taps, skip_gain, filter_spectrum, out_weight):
    devices = lax.axis_size("ctx")
    tokens, channels = query.shape
    block = channels // devices
    sent = prepared(key_in, value, short_taps, filter_spectrum, devices)
    taken = lax.all_to_all(sent, "ctx", split_axis=0, concat_axis=0, tiled=True)
    tails = own_tails(query, key_in, value)
    tails = shifted_in(tails, "ctx")
    gate_signal, direct = gates(query, key_in, value, tails, short_taps, skip_gain)
    own_taps = lax.dynamic_slice_in_dim(short_taps, lax.axis_index("ctx") * block, block, axis=2)
    tables = local_tables(tokens * devices, block)
    convolved = local_transform(taken, own_taps, tables, tokens)
    convolved = lax.all_to_all(convolved, "ctx", split_axis=0, concat_axis=0, tiled=True)
    return projected(convolved, gate_signal, direct, out_weight)


def shards(query, key_in, value, short_taps, skip_gain, filter_spectrum, out_weight):
    devices = lax.axis_size("ctx")
    tokens, channels = query.shape
    length, block = tokens * devices, channels // devices
    if block == LANES and devices == 2 * RADIX and lax.axis_size("tp") == 2:
        return fused_shards(query, key_in, value, short_taps, skip_gain, filter_spectrum, out_weight)
    tails = shifted_in(jnp.concatenate([query[-2:], key_in[-2:], value[-2:]], axis=0), "ctx")
    gate_signal = causal_filter(query, tails[0:2], short_taps[0])
    mixed_in = causal_filter(key_in, tails[2:4], short_taps[1]) * causal_filter(
        value, tails[4:6], short_taps[2]
    )
    own_signal = mixed_in.astype(jnp.bfloat16).reshape(tokens, devices, block).transpose(1, 0, 2)
    own_spectrum = (
        filter_spectrum.astype(jnp.bfloat16)
        .reshape(tokens, 2, 2, devices, block)
        .transpose(3, 2, 0, 1, 4)
        .reshape(devices, 4 * tokens, block)
    )
    sent = jnp.concatenate([own_signal, own_spectrum], axis=1)
    taken = lax.all_to_all(sent, "ctx", split_axis=0, concat_axis=0, tiled=True)
    signal = taken[:, :tokens].reshape(length, block)
    spectrum_real = taken[:, tokens : 3 * tokens].reshape(2 * length, block)
    spectrum_imag = taken[:, 3 * tokens :].reshape(2 * length, block)
    convolved = long_filter(signal, spectrum_real, spectrum_imag).astype(jnp.bfloat16)
    convolved = lax.all_to_all(
        convolved.reshape(devices, tokens, block), "ctx", split_axis=0, concat_axis=0, tiled=True
    )
    convolved = convolved.transpose(1, 0, 2).reshape(tokens, channels).astype(jnp.float32)
    gated = (gate_signal * (convolved + skip_gain * mixed_in)).astype(jnp.bfloat16)
    share = jnp.dot(gated, out_weight, preferred_element_type=jnp.float32)
    return sum_shares(share, "tp").astype(jnp.bfloat16)


def solution(mesh):
    return jax.shard_map(
        shards,
        mesh=mesh,
        in_specs=(
            P("ctx", "tp"),
            P("ctx", "tp"),
            P("ctx", "tp"),
            P(None, None, "tp"),
            P("tp"),
            P("ctx", None, None, "tp"),
            P("tp", None),
        ),
        out_specs=P("ctx", "tp"),
        check_vma=False,
    )
```

```python
import functools
import math

import jax
import jax.numpy as jnp
from jax import lax
from jax.experimental import pallas as pl
from jax.experimental.pallas import tpu as pltpu
from jax.sharding import PartitionSpec as P


RADIX = 8
ROWS = 16
LANES = 128
FAR_CHUNKS = (768, 1280)
STEP = 256
GROUP = 128
EDGE = 8


def shifted_in(rows, axis):
    count = lax.axis_size(axis)
    return lax.ppermute(rows, axis, [(i, i + 1) for i in range(count - 1)])


def causal_filter(signal, tail, taps):
    values = jnp.concatenate([tail, signal], axis=0).astype(jnp.float32)
    return taps[0] * values[2:] + taps[1] * values[1:-1] + taps[2] * values[:-2]


def turn(rows, columns, order):
    index = rows[:, None] * columns[None, :] % order
    angle = (2.0 * math.pi / order) * index.astype(jnp.float32)
    return jnp.cos(angle), jnp.sin(angle)


def exact_dot(left, right):
    return jnp.dot(left, right, precision=lax.Precision.HIGHEST, preferred_element_type=jnp.float32)


def radix_of(order):
    return 2 ** ((order.bit_length() - 1) // 2)


def long_filter(signal, spectrum_real, spectrum_imag):
    length, width = signal.shape
    order = spectrum_real.shape[0]
    radix = radix_of(order)
    span, depth = order // radix, length // radix
    low = jnp.arange(span, dtype=jnp.int32)
    deep = jnp.arange(depth, dtype=jnp.int32)
    lanes = jnp.arange(radix, dtype=jnp.int32)
    inner_cos, inner_sin = turn(low, deep, span)
    twiddle_cos, twiddle_sin = (t[:, :, None] for t in turn(lanes, low, order))
    outer_cos, outer_sin = turn(lanes, lanes, radix)

    samples = signal.astype(jnp.float32).reshape(depth, radix * width)
    real = exact_dot(inner_cos, samples).reshape(span, radix, width).transpose(1, 0, 2)
    imag = -exact_dot(inner_sin, samples).reshape(span, radix, width).transpose(1, 0, 2)
    real, imag = (
        (real * twiddle_cos + imag * twiddle_sin).reshape(radix, span * width),
        (imag * twiddle_cos - real * twiddle_sin).reshape(radix, span * width),
    )
    real, imag = (
        exact_dot(outer_cos, real) + exact_dot(outer_sin, imag),
        exact_dot(outer_cos, imag) - exact_dot(outer_sin, real),
    )
    spectrum_real = spectrum_real.astype(jnp.float32).reshape(radix, span * width)
    spectrum_imag = spectrum_imag.astype(jnp.float32).reshape(radix, span * width)
    real, imag = (
        real * spectrum_real - imag * spectrum_imag,
        real * spectrum_imag + imag * spectrum_real,
    )
    real, imag = (
        (exact_dot(outer_cos, real) - exact_dot(outer_sin, imag)).reshape(radix, span, width),
        (exact_dot(outer_cos, imag) + exact_dot(outer_sin, real)).reshape(radix, span, width),
    )
    real, imag = (
        (real * twiddle_cos - imag * twiddle_sin).transpose(1, 0, 2).reshape(span, radix * width),
        (imag * twiddle_cos + real * twiddle_sin).transpose(1, 0, 2).reshape(span, radix * width),
    )
    result = exact_dot(inner_cos.T, real) - exact_dot(inner_sin.T, imag)
    return (result / order).reshape(length, width)


def split(value):
    high = value.astype(jnp.bfloat16)
    return high, (value - high.astype(jnp.float32)).astype(jnp.bfloat16)


def filtered_block(signal_ref, tails_ref, taps_ref, which, lanes):
    values = signal_ref[:, lanes].astype(jnp.float32)
    tails = tails_ref[:, lanes].astype(jnp.float32)
    older, newer = tails[2 * which : 2 * which + 1], tails[2 * which + 1 : 2 * which + 2]
    row = lax.broadcasted_iota(jnp.int32, values.shape, 0)
    one_back = jnp.where(row == 0, newer, pltpu.roll(values, 1, 0))
    two_back = jnp.where(row == 0, older, jnp.where(row == 1, newer, pltpu.roll(values, 2, 0)))
    taps = taps_ref[which, :, lanes]
    return taps[0:1] * values + taps[1:2] * one_back + taps[2:3] * two_back


def tails_kernel(query_ref, key_ref, value_ref, tails_ref):
    rows = query_ref.shape[0]
    for which, ref in enumerate((query_ref, key_ref, value_ref)):
        tails_ref[2 * which : 2 * which + 2, :] = ref[...].astype(jnp.float32)[rows - 2 :].astype(jnp.bfloat16)


def own_tails(query, key_in, value):
    tokens, channels = query.shape
    last = pl.BlockSpec((ROWS, channels), lambda i: (tokens // ROWS - 1, 0))
    return pl.pallas_call(
        tails_kernel,
        grid=(1,),
        out_shape=jax.ShapeDtypeStruct((6, channels), query.dtype),
        in_specs=[last] * 3,
        out_specs=pl.BlockSpec((6, channels), lambda i: (0, 0)),
        compiler_params=pltpu.CompilerParams(vmem_limit_bytes=4 * 2**20),
    )(*(pltpu.with_memory_space_constraint(a, pltpu.HBM) for a in (query, key_in, value)))


def gather_rows(size, count, invert=False):
    row = lax.broadcasted_iota(jnp.int32, (size, size), 0)
    column = lax.broadcasted_iota(jnp.int32, (size, size), 1)
    if invert:
        row, column = column, row
    inner = size // count
    match = column == (row % inner) * count + row // inner
    return jnp.where(match, 1.0, 0.0).astype(jnp.bfloat16)


def exact_rows(matrix, left, right):
    both = jnp.concatenate([left, right], axis=1)
    return jnp.dot(matrix, both, preferred_element_type=jnp.float32).astype(jnp.bfloat16)


def unshifted(values, taps):
    return taps[0:1] * values + taps[1:2] * pltpu.roll(values, 1, 0) + taps[2:3] * pltpu.roll(values, 2, 0)


def prepare_kernel(spectrum_ref, key_ref, value_ref, taps_ref, sent_ref, *scratch):
    spectrum, key, value, taps, staged, in_sems, out_sems = scratch
    devices, _, block = staged.shape
    tokens = key.shape[0]
    fine = 2 * devices
    slab = GROUP * fine
    groups = spectrum.shape[0] // slab
    loads = [
        pltpu.make_async_copy(source, target, in_sems.at[i])
        for i, (source, target) in enumerate(((taps_ref, taps), (key_ref, key), (value_ref, value)))
    ] + [
        pltpu.make_async_copy(
            spectrum_ref.at[pl.ds(g * slab, slab)], spectrum.at[pl.ds(g * slab, slab)], in_sems.at[3 + g]
        )
        for g in range(groups)
    ]
    for load in loads:
        load.start()
    stores = []

    def store(start, size):
        rows = pl.ds(start, size)
        stores.append(
            pltpu.make_async_copy(staged.at[:, rows], sent_ref.at[:, rows], out_sems.at[len(stores)])
        )
        stores[-1].start()

    for load in loads[:3]:
        load.wait()
    edge = tokens + 2 * GROUP * groups
    for j in range(devices):
        lanes = pl.ds(j * block, block)
        k, v = key[:, lanes].astype(jnp.float32), value[:, lanes].astype(jnp.float32)
        mixed = unshifted(k, taps[1, :, lanes]) * unshifted(v, taps[2, :, lanes])
        staged[j, pl.ds(0, tokens), :] = mixed.astype(jnp.bfloat16)
        ends = jnp.concatenate([k[:2], v[:2], k[tokens - 2 :], v[tokens - 2 :]], axis=0)
        staged[j, pl.ds(edge, EDGE), :] = ends.astype(jnp.bfloat16)
    store(0, tokens)
    store(edge, EDGE)

    matrix = gather_rows(EDGE * fine, fine)
    for g in range(groups):
        loads[3 + g].wait()
        start = tokens + 2 * GROUP * g
        for h in range(0, GROUP, 2 * EDGE):
            slabs = [
                spectrum[pl.ds((g * GROUP + h + p) * fine, EDGE * fine), :].astype(jnp.bfloat16)
                for p in (0, EDGE)
            ]
            both = exact_rows(matrix, *slabs)
            for s in range(fine):
                rows = both[s * EDGE : (s + 1) * EDGE]
                pair = jnp.concatenate([rows[:, :block], rows[:, block:]], axis=0)
                staged[s // 2, pl.ds(start + s % 2 * GROUP + h, 2 * EDGE), :] = pair
        store(start, 2 * GROUP)
    for copy in stores:
        copy.wait()


def prepared(key_in, value, short_taps, filter_spectrum, devices):
    tokens, _, _, channels = filter_spectrum.shape
    block, pairs = channels // devices, 2 * tokens
    groups = pairs // GROUP
    view = (
        filter_spectrum.reshape(tokens, 2, 2, devices, block)
        .transpose(0, 1, 3, 2, 4)
        .reshape(2 * pairs * devices, block)
    )
    rows = tokens + 2 * pairs + EDGE
    remote = pl.BlockSpec(memory_space=pltpu.HBM)
    inputs = [
        pltpu.with_memory_space_constraint(a, pltpu.HBM) for a in (view, key_in, value, short_taps)
    ]
    return pl.pallas_call(
        prepare_kernel,
        out_shape=pltpu.HBM((devices, rows, block), jnp.bfloat16),
        in_specs=[remote] * 4,
        out_specs=remote,
        scratch_shapes=[
            pltpu.VMEM(view.shape, jnp.float32),
            pltpu.VMEM((tokens, channels), jnp.bfloat16),
            pltpu.VMEM((tokens, channels), jnp.bfloat16),
            pltpu.VMEM(short_taps.shape, jnp.float32),
            pltpu.VMEM((devices, rows, block), jnp.bfloat16),
            pltpu.SemaphoreType.DMA((3 + groups,)),
            pltpu.SemaphoreType.DMA((2 + groups,)),
        ],
        compiler_params=pltpu.CompilerParams(vmem_limit_bytes=20 * 2**20),
        cost_estimate=pl.CostEstimate(flops=0, bytes_accessed=view.size * 6, transcendentals=0),
    )(*inputs)


def gate_kernel(tails_ref, *refs):
    sources, (gate_ref, direct_ref), held, sems = refs[:5], refs[5:7], refs[7:12], refs[12]
    query_ref, key_ref, value_ref, taps_ref, gain_ref = held
    loads = [
        pltpu.make_async_copy(source, target, sems.at[i])
        for i, (source, target) in enumerate(zip(sources, held))
    ]
    for load in loads:
        load.start()
    for load in loads:
        load.wait()
    _, channels = query_ref.shape
    for j in range(channels // LANES):
        lanes = pl.ds(j * LANES, LANES)
        mixed = filtered_block(key_ref, tails_ref, taps_ref, 1, lanes) * filtered_block(
            value_ref, tails_ref, taps_ref, 2, lanes
        )
        gate_ref[:, lanes] = filtered_block(query_ref, tails_ref, taps_ref, 0, lanes)
        direct_ref[:, lanes] = gain_ref[:, lanes] * mixed


def gates(query, key_in, value, tails, short_taps, skip_gain):
    shape = jax.ShapeDtypeStruct(query.shape, jnp.float32)
    whole, remote = pl.BlockSpec(memory_space=pltpu.VMEM), pl.BlockSpec(memory_space=pltpu.HBM)
    inputs = [query, key_in, value, short_taps, skip_gain[None, :]]
    return pl.pallas_call(
        gate_kernel,
        out_shape=(shape, shape),
        in_specs=[whole] + [remote] * len(inputs),
        out_specs=(whole, whole),
        scratch_shapes=[
            *(pltpu.VMEM(a.shape, a.dtype) for a in inputs),
            pltpu.SemaphoreType.DMA((len(inputs),)),
        ],
        compiler_params=pltpu.CompilerParams(vmem_limit_bytes=16 * 2**20),
        cost_estimate=pl.CostEstimate(
            flops=20 * query.size, bytes_accessed=14 * query.size, transcendentals=0
        ),
    )(tails, *(pltpu.with_memory_space_constraint(a, pltpu.HBM) for a in inputs))


def column_copies(weight_ref, held, sems, first):
    chunks, _, width = held.shape
    return [
        pltpu.make_async_copy(
            weight_ref.at[:, pl.ds(pl.multiple_of(first + i * width, LANES), width)],
            held.at[i],
            sems.at[i],
        )
        for i in range(chunks)
    ]


def multiply(gated_ref, share_ref, held, copies):
    width = held.shape[2]
    for i, copy in enumerate(copies):
        copy.wait()
        share_ref[:, pl.ds(i * width, width)] = jnp.dot(
            gated_ref[...], held[i], preferred_element_type=jnp.float32
        ).astype(share_ref.dtype)


def gated_kernel(conv_ref, gate_ref, direct_ref, weight_ref, gated_ref, share_ref, held, sems):
    devices, _, block = conv_ref.shape
    columns = weight_ref.shape[1] // 2
    copies = column_copies(weight_ref, held, sems, (1 - lax.axis_index("tp")) * columns)
    for copy in copies:
        copy.start()
    for j in range(devices):
        lanes = pl.ds(j * block, block)
        gated_ref[:, lanes] = (
            gate_ref[:, lanes] * (conv_ref[j].astype(jnp.float32) + direct_ref[:, lanes])
        ).astype(jnp.bfloat16)
    multiply(gated_ref, share_ref, held, copies)


def share_kernel(far, offset, gated_ref, weight_ref, share_ref, held, sems):
    columns = weight_ref.shape[1] // 2
    rank = lax.axis_index("tp")
    copies = column_copies(weight_ref, held, sems, (1 - rank if far else rank) * columns + offset)
    for copy in copies:
        copy.start()
    multiply(gated_ref, share_ref, held, copies)


def projected(convolved, gate_signal, direct, out_weight):
    tokens, channels = gate_signal.shape
    columns = out_weight.shape[1] // 2
    whole, remote = pl.BlockSpec(memory_space=pltpu.VMEM), pl.BlockSpec(memory_space=pltpu.HBM)
    out_weight = pltpu.with_memory_space_constraint(out_weight, pltpu.HBM)

    def share(kernel, operands, extra, width, step, dtype):
        return pl.pallas_call(
            kernel,
            out_shape=(*extra, jax.ShapeDtypeStruct((tokens, width), dtype)),
            in_specs=[whole] * len(operands) + [remote],
            out_specs=(whole,) * (len(extra) + 1),
            scratch_shapes=[
                pltpu.VMEM((width // step, channels, step), jnp.bfloat16),
                pltpu.SemaphoreType.DMA((width // step,)),
            ],
            compiler_params=pltpu.CompilerParams(vmem_limit_bytes=20 * 2**20),
            cost_estimate=pl.CostEstimate(
                flops=2 * tokens * channels * width, bytes_accessed=2 * channels * width, transcendentals=0
            ),
        )(*operands, out_weight)

    swap = [(0, 1), (1, 0)]
    widths = FAR_CHUNKS if sum(FAR_CHUNKS) == columns else (columns,)
    arrived, offset, gated = [], 0, None
    for width in widths:
        if gated is None:
            gated, far = share(
                gated_kernel,
                (convolved, gate_signal, direct),
                (jax.ShapeDtypeStruct((tokens, channels), jnp.bfloat16),),
                width,
                STEP,
                jnp.bfloat16,
            )
        else:
            kernel = functools.partial(share_kernel, True, offset)
            (far,) = share(kernel, (gated,), (), width, STEP, jnp.bfloat16)
        arrived.append(lax.ppermute(far, "tp", swap))
        offset += width
    kernel = functools.partial(share_kernel, False, 0)
    (near,) = share(kernel, (gated,), (), columns, 2 * STEP, jnp.float32)
    return (near + jnp.concatenate(arrived, axis=1).astype(jnp.float32)).astype(jnp.bfloat16)


def butterfly(parts, sign):
    count = len(parts)
    if count == 1:
        return parts
    even, odd = butterfly(parts[0::2], sign), butterfly(parts[1::2], sign)
    half = count // 2
    low, high = [], []
    for j in range(half):
        real, imag = odd[j]
        if 4 * j == count:
            real, imag = (-imag, real) if sign > 0 else (imag, -real)
        elif j:
            c, s = math.cos(2.0 * math.pi * j / count), sign * math.sin(2.0 * math.pi * j / count)
            if 8 * j == count:
                real, imag = ((real - imag) * c, (real + imag) * c) if sign > 0 else ((real + imag) * c, (imag - real) * c)
            elif 8 * j == 3 * count:
                real, imag = ((real + imag) * c, (imag - real) * c) if sign > 0 else ((real - imag) * c, (real + imag) * c)
            else:
                real, imag = real * c - imag * s, real * s + imag * c
        low.append((even[j][0] + real, even[j][1] + imag))
        high.append((even[j][0] - real, even[j][1] - imag))
    return low + high


def turned(pair, cosine, sine):
    real, imag = pair
    return real * cosine - imag * sine, imag * cosine + real * sine


def scaled(pair, factor):
    return turned(pair, *factor)


def powers_of(root):
    powers = [None, root]
    for v in range(2, RADIX):
        powers.append(turned(powers[v // 2], *powers[v - v // 2]))
    return powers


def transform_kernel(
    taken_ref, taps_ref, forward, cos_ref, sin_ref, inverse, out_ref,
    result_ref, packed, inner, flipped, high_ref, low_ref, done, sems, edges,
):
    devices, tokens, block = done.shape
    half = cos_ref.shape[0]
    lane = [pl.ds(v * block, block) for v in range(RADIX)]
    edge = tokens + 2 * half

    edges[:EDGE] = jnp.zeros((EDGE, block), jnp.float32)
    for q in range(devices):
        edges[pl.ds((q + 1) * EDGE, EDGE)] = taken_ref[q, pl.ds(edge, EDGE), :].astype(jnp.float32)

    def ends(index, own):
        return edges[pl.ds(index + EDGE * own, devices, stride=EDGE), :]

    def first_rows(which):
        taps = taps_ref[which]
        base = 2 * (which - 1)
        now, after = ends(base, 1), ends(base + 1, 1)
        older, newer = ends(base + 4, 0), ends(base + 5, 0)
        return (
            taps[0:1] * now + taps[1:2] * newer + taps[2:3] * older,
            taps[0:1] * after + taps[1:2] * now + taps[2:3] * newer,
        )

    key_rows, value_rows = first_rows(1), first_rows(2)
    first_row, second_row = key_rows[0] * value_rows[0], key_rows[1] * value_rows[1]

    def tokens_of(q):
        top = taken_ref[q, pl.ds(0, ROWS), :].astype(jnp.float32)
        index = lax.broadcasted_iota(jnp.int32, top.shape, 0)
        top = jnp.where(index == 0, first_row[q : q + 1], jnp.where(index == 1, second_row[q : q + 1], top))
        return jnp.concatenate(
            [top.astype(jnp.bfloat16), taken_ref[q, pl.ds(ROWS, tokens - ROWS), :]], axis=0
        )

    def spectrum_rows(start, imag):
        return pl.ds(tokens + start // GROUP * 2 * GROUP + start % GROUP + imag * GROUP, ROWS)

    part = half // RADIX
    matrix = gather_rows(half, RADIX)
    for k in range(0, RADIX, 2):
        slabs = [tokens_of(2 * k + q) for q in range(4)]
        both = exact_rows(
            matrix, jnp.concatenate(slabs[:2], axis=0), jnp.concatenate(slabs[2:], axis=0)
        )
        for v in range(RADIX):
            rows = both[v * part : (v + 1) * part]
            packed[pl.ds(k * part, part), lane[v]] = rows[:, :block]
            packed[pl.ds((k + 1) * part, part), lane[v]] = rows[:, block:]

    row = lax.broadcasted_iota(jnp.int32, (half, half), 0)
    column = lax.broadcasted_iota(jnp.int32, (half, half), 1)
    flip = jnp.where(row + column == half, 1.0, 0.0).astype(jnp.bfloat16)
    for j in range(RADIX):
        source = 2 * RADIX - 1 - 2 * j
        right = jnp.concatenate(
            [
                jnp.concatenate(
                    [
                        taken_ref[source, pl.ds(tokens + (2 * g + imag) * GROUP, GROUP), :]
                        for g in range(half // GROUP)
                    ],
                    axis=0,
                )
                for imag in range(2)
            ],
            axis=1,
        )
        flipped[j] = jnp.dot(flip, right, preferred_element_type=jnp.float32).astype(jnp.bfloat16)

    wide = 2 * block
    for v in range(0, RADIX, 2):
        lanes = pl.ds(v * block, wide)
        right = packed[:, lanes]
        inner[:, lanes] = jnp.dot(forward[...], right, preferred_element_type=jnp.float32)

    def products(rows, start, parts):
        parts = butterfly(parts, -1)
        result = []
        for j in range(RADIX):
            real = taken_ref[2 * j, spectrum_rows(start, 0), :].astype(jnp.float32)
            imag = taken_ref[2 * j, spectrum_rows(start, 1), :].astype(jnp.float32)
            mirror = flipped[j, rows, :].astype(jnp.float32)
            result.append(scaled(parts[j], (real + mirror[:, :block], imag - mirror[:, block:])))
        return butterfly(result, 1)

    def middle(start, first):
        rows = pl.ds(start, ROWS)
        rows_imag = pl.ds(start + half, ROWS)
        top = lax.broadcasted_iota(jnp.int32, (ROWS, block), 0) == 0
        powers = powers_of((cos_ref[rows, :], sin_ref[rows, :]))
        parts, tops = [], []
        for v in range(RADIX):
            real, imag = inner[rows, lane[v]], -inner[rows_imag, lane[v]]
            if first:
                tops.append(-imag)
                imag = jnp.where(top, 0.0, imag)
            if v:
                cosine, sine = powers[v]
                real, imag = turned((real, imag), cosine, -sine)
            parts.append((real, imag))
        parts = products(rows, start, parts)
        if first:
            angles = [math.pi * v / RADIX for v in range(RADIX)]
            nyquist = [(t * math.cos(a), t * -math.sin(a)) for t, a in zip(tops, angles)]
            nyquist = butterfly(nyquist, -1)
            nyquist = [
                scaled(
                    nyquist[j],
                    (
                        taken_ref[2 * j + 1, spectrum_rows(0, 0), :].astype(jnp.float32),
                        taken_ref[2 * j + 1, spectrum_rows(0, 1), :].astype(jnp.float32),
                    ),
                )
                for j in range(RADIX)
            ]
            nyquist = butterfly(nyquist, 1)
            tops = [n[0] * math.cos(a) - n[1] * math.sin(a) for n, a in zip(nyquist, angles)]
        for v in range(RADIX):
            real, imag = parts[v]
            if v:
                real, imag = turned((real, imag), *powers[v])
            imag = jnp.where(top, tops[v], -imag) if first else -imag
            high_ref[rows, lane[v]], low_ref[rows, lane[v]] = split(real)
            high_ref[rows_imag, lane[v]], low_ref[rows_imag, lane[v]] = split(imag)

    middle(0, True)

    @pl.loop(1, half // ROWS)
    def _(i):
        middle(pl.multiple_of(i * ROWS, ROWS), False)

    for v in range(0, RADIX, 2):
        lanes = pl.ds(v * block, wide)
        right = high_ref[:, lanes]
        result = (
            jnp.dot(inverse[...], right, preferred_element_type=jnp.float32)
            + jnp.dot(inverse[...], low_ref[:, lanes], preferred_element_type=jnp.float32)
        ) * (0.5 / (devices * tokens))
        result_ref[:, lanes] = result.astype(jnp.bfloat16)

    matrix = gather_rows(half, RADIX, invert=True)
    copies = []
    for k in range(0, RADIX, 2):
        slabs = [
            jnp.concatenate([result_ref[pl.ds(p * part, part), lane[v]] for v in range(RADIX)], axis=0)
            for p in (k, k + 1)
        ]
        both = exact_rows(matrix, *slabs)
        for q in range(4):
            done[2 * k + q] = both[(q % 2) * tokens : (q % 2 + 1) * tokens, (q // 2) * block : (q // 2 + 1) * block]
        copies.append(
            pltpu.make_async_copy(
                done.at[pl.ds(2 * k, 4)], out_ref.at[pl.ds(2 * k, 4)], sems.at[k // 2]
            )
        )
        copies[-1].start()
    for copy in copies:
        copy.wait()


def angles_of(shape, rows, columns, order):
    index = lax.broadcasted_iota(jnp.int32, shape, rows) * lax.broadcasted_iota(jnp.int32, shape, columns)
    return (2.0 * math.pi / order) * (index & (order - 1)).astype(jnp.float32)


def tables_kernel(forward, cos_ref, sin_ref, inverse):
    depth = forward.shape[1]
    half, block = cos_ref.shape
    order = 2 * RADIX * half

    def alternating(shape, dim):
        return (1 - 2 * (lax.broadcasted_iota(jnp.int32, shape, dim) & 1)).astype(jnp.float32)

    def first(shape, dim):
        return lax.broadcasted_iota(jnp.int32, shape, dim) == 0

    shape = (half, depth)
    angle = angles_of(shape, 0, 1, 2 * half)
    forward[:half] = jnp.cos(angle).astype(jnp.bfloat16)
    sine = jnp.where(first(shape, 0), alternating(shape, 1), jnp.sin(angle))
    forward[half:] = sine.astype(jnp.bfloat16)
    shape = (depth, half)
    angle = angles_of(shape, 0, 1, 2 * half)
    inverse[:, :half] = jnp.cos(angle).astype(jnp.bfloat16)
    sine = jnp.where(first(shape, 1), alternating(shape, 0), jnp.sin(angle))
    inverse[:, half:] = sine.astype(jnp.bfloat16)

    step = lax.broadcasted_iota(jnp.int32, (half, block), 0).astype(jnp.float32)
    angle = (2.0 * math.pi / order) * step
    cos_ref[...] = jnp.cos(angle)
    sin_ref[...] = jnp.sin(angle)


def local_tables(length, block):
    half, depth = length // RADIX, length // RADIX
    whole = pl.BlockSpec(memory_space=pltpu.VMEM)
    forward = jax.ShapeDtypeStruct((2 * half, depth), jnp.bfloat16)
    inverse = jax.ShapeDtypeStruct((depth, 2 * half), jnp.bfloat16)
    twiddle = jax.ShapeDtypeStruct((half, block), jnp.float32)
    return pl.pallas_call(
        tables_kernel,
        out_shape=(forward, twiddle, twiddle, inverse),
        out_specs=(whole,) * 4,
        compiler_params=pltpu.CompilerParams(vmem_limit_bytes=16 * 2**20),
        cost_estimate=pl.CostEstimate(
            flops=200 * RADIX * half * block, bytes_accessed=8 * RADIX * half * block, transcendentals=0
        ),
    )()


def local_transform(taken, taps, tables, tokens):
    devices, _, block = taken.shape
    length = devices * tokens
    half, depth = length // RADIX, length // RADIX
    flops = 3 * 2 * 2 * half * depth * RADIX * block
    whole, remote = pl.BlockSpec(memory_space=pltpu.VMEM), pl.BlockSpec(memory_space=pltpu.HBM)
    wide = RADIX * block
    return pl.pallas_call(
        transform_kernel,
        out_shape=pltpu.HBM((devices, tokens, block), jnp.bfloat16),
        in_specs=[whole] * 6,
        out_specs=remote,
        scratch_shapes=[
            pltpu.VMEM((depth, wide), jnp.bfloat16),
            pltpu.VMEM((depth, wide), jnp.bfloat16),
            pltpu.VMEM((2 * half, wide), jnp.float32),
            pltpu.VMEM((RADIX, half, 2 * block), jnp.bfloat16),
            pltpu.VMEM((2 * half, wide), jnp.bfloat16),
            pltpu.VMEM((2 * half, wide), jnp.bfloat16),
            pltpu.VMEM((devices, tokens, block), jnp.bfloat16),
            pltpu.SemaphoreType.DMA((RADIX // 2,)),
            pltpu.VMEM(((devices + 1) * EDGE, block), jnp.float32),
        ],
        compiler_params=pltpu.CompilerParams(vmem_limit_bytes=20 * 2**20),
        cost_estimate=pl.CostEstimate(flops=flops, bytes_accessed=taken.size * 2, transcendentals=0),
    )(taken, taps, *tables)


def sum_shares(share, axis):
    count = lax.axis_size(axis)
    rank = lax.axis_index(axis)
    columns = share.shape[1] // count
    total = lax.dynamic_slice_in_dim(share, rank * columns, columns, axis=1)
    for step in range(1, count):
        piece = lax.dynamic_slice_in_dim(share, (rank + step) % count * columns, columns, axis=1)
        pairs = [(i, (i + step) % count) for i in range(count)]
        total = total + lax.ppermute(piece.astype(jnp.bfloat16), axis, pairs).astype(jnp.float32)
    return total


def fused_shards(query, key_in, value, short_taps, skip_gain, filter_spectrum, out_weight):
    devices = lax.axis_size("ctx")
    tokens, channels = query.shape
    block = channels // devices
    sent = prepared(key_in, value, short_taps, filter_spectrum, devices)
    taken = lax.all_to_all(sent, "ctx", split_axis=0, concat_axis=0, tiled=True)
    tails = own_tails(query, key_in, value)
    tails = shifted_in(tails, "ctx")
    gate_signal, direct = gates(query, key_in, value, tails, short_taps, skip_gain)
    own_taps = lax.dynamic_slice_in_dim(short_taps, lax.axis_index("ctx") * block, block, axis=2)
    tables = local_tables(tokens * devices, block)
    convolved = local_transform(taken, own_taps, tables, tokens)
    convolved = lax.all_to_all(convolved, "ctx", split_axis=0, concat_axis=0, tiled=True)
    return projected(convolved, gate_signal, direct, out_weight)


def shards(query, key_in, value, short_taps, skip_gain, filter_spectrum, out_weight):
    devices = lax.axis_size("ctx")
    tokens, channels = query.shape
    length, block = tokens * devices, channels // devices
    if block == LANES and devices == 2 * RADIX and lax.axis_size("tp") == 2:
        return fused_shards(query, key_in, value, short_taps, skip_gain, filter_spectrum, out_weight)
    tails = shifted_in(jnp.concatenate([query[-2:], key_in[-2:], value[-2:]], axis=0), "ctx")
    gate_signal = causal_filter(query, tails[0:2], short_taps[0])
    mixed_in = causal_filter(key_in, tails[2:4], short_taps[1]) * causal_filter(
        value, tails[4:6], short_taps[2]
    )
    own_signal = mixed_in.astype(jnp.bfloat16).reshape(tokens, devices, block).transpose(1, 0, 2)
    own_spectrum = (
        filter_spectrum.astype(jnp.bfloat16)
        .reshape(tokens, 2, 2, devices, block)
        .transpose(3, 2, 0, 1, 4)
        .reshape(devices, 4 * tokens, block)
    )
    sent = jnp.concatenate([own_signal, own_spectrum], axis=1)
    taken = lax.all_to_all(sent, "ctx", split_axis=0, concat_axis=0, tiled=True)
    signal = taken[:, :tokens].reshape(length, block)
    spectrum_real = taken[:, tokens : 3 * tokens].reshape(2 * length, block)
    spectrum_imag = taken[:, 3 * tokens :].reshape(2 * length, block)
    convolved = long_filter(signal, spectrum_real, spectrum_imag).astype(jnp.bfloat16)
    convolved = lax.all_to_all(
        convolved.reshape(devices, tokens, block), "ctx", split_axis=0, concat_axis=0, tiled=True
    )
    convolved = convolved.transpose(1, 0, 2).reshape(tokens, channels).astype(jnp.float32)
    gated = (gate_signal * (convolved + skip_gain * mixed_in)).astype(jnp.bfloat16)
    share = jnp.dot(gated, out_weight, preferred_element_type=jnp.float32)
    return sum_shares(share, "tp").astype(jnp.bfloat16)


def solution(mesh):
    return jax.shard_map(
        shards,
        mesh=mesh,
        in_specs=(
            P("ctx", "tp"),
            P("ctx", "tp"),
            P("ctx", "tp"),
            P(None, None, "tp"),
            P("tp"),
            P("ctx", None, None, "tp"),
            P("tp", None),
        ),
        out_specs=P("ctx", "tp"),
        check_vma=False,
    )
```

```python
import functools
import math

import jax
import jax.numpy as jnp
from jax import lax
from jax.experimental import pallas as pl
from jax.experimental.pallas import tpu as pltpu
from jax.sharding import PartitionSpec as P


RADIX = 8
ROWS = 16
LANES = 128
FAR_CHUNKS = (512, 768, 768)
STEP = 256
GROUP = 64
EDGE = 8


def shifted_in(rows, axis):
    count = lax.axis_size(axis)
    return lax.ppermute(rows, axis, [(i, i + 1) for i in range(count - 1)])


def causal_filter(signal, tail, taps):
    values = jnp.concatenate([tail, signal], axis=0).astype(jnp.float32)
    return taps[0] * values[2:] + taps[1] * values[1:-1] + taps[2] * values[:-2]


def turn(rows, columns, order):
    index = rows[:, None] * columns[None, :] % order
    angle = (2.0 * math.pi / order) * index.astype(jnp.float32)
    return jnp.cos(angle), jnp.sin(angle)


def exact_dot(left, right):
    return jnp.dot(left, right, precision=lax.Precision.HIGHEST, preferred_element_type=jnp.float32)


def radix_of(order):
    return 2 ** ((order.bit_length() - 1) // 2)


def long_filter(signal, spectrum_real, spectrum_imag):
    length, width = signal.shape
    order = spectrum_real.shape[0]
    radix = radix_of(order)
    span, depth = order // radix, length // radix
    low = jnp.arange(span, dtype=jnp.int32)
    deep = jnp.arange(depth, dtype=jnp.int32)
    lanes = jnp.arange(radix, dtype=jnp.int32)
    inner_cos, inner_sin = turn(low, deep, span)
    twiddle_cos, twiddle_sin = (t[:, :, None] for t in turn(lanes, low, order))
    outer_cos, outer_sin = turn(lanes, lanes, radix)

    samples = signal.astype(jnp.float32).reshape(depth, radix * width)
    real = exact_dot(inner_cos, samples).reshape(span, radix, width).transpose(1, 0, 2)
    imag = -exact_dot(inner_sin, samples).reshape(span, radix, width).transpose(1, 0, 2)
    real, imag = (
        (real * twiddle_cos + imag * twiddle_sin).reshape(radix, span * width),
        (imag * twiddle_cos - real * twiddle_sin).reshape(radix, span * width),
    )
    real, imag = (
        exact_dot(outer_cos, real) + exact_dot(outer_sin, imag),
        exact_dot(outer_cos, imag) - exact_dot(outer_sin, real),
    )
    spectrum_real = spectrum_real.astype(jnp.float32).reshape(radix, span * width)
    spectrum_imag = spectrum_imag.astype(jnp.float32).reshape(radix, span * width)
    real, imag = (
        real * spectrum_real - imag * spectrum_imag,
        real * spectrum_imag + imag * spectrum_real,
    )
    real, imag = (
        (exact_dot(outer_cos, real) - exact_dot(outer_sin, imag)).reshape(radix, span, width),
        (exact_dot(outer_cos, imag) + exact_dot(outer_sin, real)).reshape(radix, span, width),
    )
    real, imag = (
        (real * twiddle_cos - imag * twiddle_sin).transpose(1, 0, 2).reshape(span, radix * width),
        (imag * twiddle_cos + real * twiddle_sin).transpose(1, 0, 2).reshape(span, radix * width),
    )
    result = exact_dot(inner_cos.T, real) - exact_dot(inner_sin.T, imag)
    return (result / order).reshape(length, width)


def split(value):
    high = value.astype(jnp.bfloat16)
    return high, (value - high.astype(jnp.float32)).astype(jnp.bfloat16)


def filtered_block(signal_ref, tails_ref, taps_ref, which, lanes):
    values = signal_ref[:, lanes].astype(jnp.float32)
    tails = tails_ref[:, lanes].astype(jnp.float32)
    older, newer = tails[2 * which : 2 * which + 1], tails[2 * which + 1 : 2 * which + 2]
    row = lax.broadcasted_iota(jnp.int32, values.shape, 0)
    one_back = jnp.where(row == 0, newer, pltpu.roll(values, 1, 0))
    two_back = jnp.where(row == 0, older, jnp.where(row == 1, newer, pltpu.roll(values, 2, 0)))
    taps = taps_ref[which, :, lanes]
    return taps[0:1] * values + taps[1:2] * one_back + taps[2:3] * two_back


def tails_kernel(query_ref, key_ref, value_ref, tails_ref):
    rows = query_ref.shape[0]
    for which, ref in enumerate((query_ref, key_ref, value_ref)):
        tails_ref[2 * which : 2 * which + 2, :] = ref[...].astype(jnp.float32)[rows - 2 :].astype(jnp.bfloat16)


def own_tails(query, key_in, value):
    tokens, channels = query.shape
    last = pl.BlockSpec((ROWS, channels), lambda i: (tokens // ROWS - 1, 0))
    return pl.pallas_call(
        tails_kernel,
        grid=(1,),
        out_shape=jax.ShapeDtypeStruct((6, channels), query.dtype),
        in_specs=[last] * 3,
        out_specs=pl.BlockSpec((6, channels), lambda i: (0, 0)),
        compiler_params=pltpu.CompilerParams(vmem_limit_bytes=4 * 2**20),
    )(*(pltpu.with_memory_space_constraint(a, pltpu.HBM) for a in (query, key_in, value)))


def gather_rows(size, count, invert=False):
    row = lax.broadcasted_iota(jnp.int32, (size, size), 0)
    column = lax.broadcasted_iota(jnp.int32, (size, size), 1)
    if invert:
        row, column = column, row
    inner = size // count
    match = column == (row % inner) * count + row // inner
    return jnp.where(match, 1.0, 0.0).astype(jnp.bfloat16)


def exact_rows(matrix, left, right):
    both = jnp.concatenate([left, right], axis=1)
    return jnp.dot(matrix, both, preferred_element_type=jnp.float32).astype(jnp.bfloat16)


def unshifted(values, taps):
    return taps[0:1] * values + taps[1:2] * pltpu.roll(values, 1, 0) + taps[2:3] * pltpu.roll(values, 2, 0)


def prepare_kernel(spectrum_ref, key_ref, value_ref, taps_ref, sent_ref, *scratch):
    spectrum, key, value, taps, staged, in_sems, out_sems = scratch
    devices, _, block = staged.shape
    tokens = key.shape[0]
    fine = 2 * devices
    slab = GROUP * fine
    groups = spectrum.shape[0] // slab
    loads = [
        pltpu.make_async_copy(source, target, in_sems.at[i])
        for i, (source, target) in enumerate(((taps_ref, taps), (key_ref, key), (value_ref, value)))
    ] + [
        pltpu.make_async_copy(
            spectrum_ref.at[pl.ds(g * slab, slab)], spectrum.at[pl.ds(g * slab, slab)], in_sems.at[3 + g]
        )
        for g in range(groups)
    ]
    for load in loads:
        load.start()
    stores = []

    def store(start, size):
        rows = pl.ds(start, size)
        stores.append(
            pltpu.make_async_copy(staged.at[:, rows], sent_ref.at[:, rows], out_sems.at[len(stores)])
        )
        stores[-1].start()

    for load in loads[:3]:
        load.wait()
    edge = tokens + 2 * GROUP * groups
    order = gather_rows(tokens, RADIX)

    def mixed(j):
        lanes = pl.ds(j * block, block)
        k, v = key[:, lanes].astype(jnp.float32), value[:, lanes].astype(jnp.float32)
        ends = jnp.concatenate([k[:2], v[:2], k[tokens - 2 :], v[tokens - 2 :]], axis=0)
        staged[j, pl.ds(edge, EDGE), :] = ends.astype(jnp.bfloat16)
        product = unshifted(k, taps[1, :, lanes]) * unshifted(v, taps[2, :, lanes])
        return product.astype(jnp.bfloat16)

    for j in range(0, devices, 2):
        both = exact_rows(order, mixed(j), mixed(j + 1))
        staged[j, pl.ds(0, tokens), :] = both[:, :block]
        staged[j + 1, pl.ds(0, tokens), :] = both[:, block:]
    store(0, tokens)
    store(edge, EDGE)

    matrix = gather_rows(EDGE * fine, fine)
    for g in range(groups):
        loads[3 + g].wait()
        start = tokens + 2 * GROUP * g
        for h in range(0, GROUP, 2 * EDGE):
            slabs = [
                spectrum[pl.ds((g * GROUP + h + p) * fine, EDGE * fine), :].astype(jnp.bfloat16)
                for p in (0, EDGE)
            ]
            both = exact_rows(matrix, *slabs)
            for s in range(fine):
                rows = both[s * EDGE : (s + 1) * EDGE]
                pair = jnp.concatenate([rows[:, :block], rows[:, block:]], axis=0)
                staged[s // 2, pl.ds(start + s % 2 * GROUP + h, 2 * EDGE), :] = pair
        store(start, 2 * GROUP)
    for copy in stores:
        copy.wait()


def prepared(key_in, value, short_taps, filter_spectrum, devices):
    tokens, _, _, channels = filter_spectrum.shape
    block, pairs = channels // devices, 2 * tokens
    groups = pairs // GROUP
    view = (
        filter_spectrum.reshape(tokens, 2, 2, devices, block)
        .transpose(0, 1, 3, 2, 4)
        .reshape(2 * pairs * devices, block)
    )
    rows = tokens + 2 * pairs + EDGE
    remote = pl.BlockSpec(memory_space=pltpu.HBM)
    inputs = [
        pltpu.with_memory_space_constraint(a, pltpu.HBM) for a in (view, key_in, value, short_taps)
    ]
    return pl.pallas_call(
        prepare_kernel,
        out_shape=pltpu.HBM((devices, rows, block), jnp.bfloat16),
        in_specs=[remote] * 4,
        out_specs=remote,
        scratch_shapes=[
            pltpu.VMEM(view.shape, jnp.float32),
            pltpu.VMEM((tokens, channels), jnp.bfloat16),
            pltpu.VMEM((tokens, channels), jnp.bfloat16),
            pltpu.VMEM(short_taps.shape, jnp.float32),
            pltpu.VMEM((devices, rows, block), jnp.bfloat16),
            pltpu.SemaphoreType.DMA((3 + groups,)),
            pltpu.SemaphoreType.DMA((2 + groups,)),
        ],
        compiler_params=pltpu.CompilerParams(vmem_limit_bytes=20 * 2**20),
        cost_estimate=pl.CostEstimate(flops=0, bytes_accessed=view.size * 6, transcendentals=0),
    )(*inputs)


def gate_kernel(tails_ref, *refs):
    sources, (gate_ref, direct_ref), held, sems = refs[:5], refs[5:7], refs[7:12], refs[12]
    query_ref, key_ref, value_ref, taps_ref, gain_ref = held
    loads = [
        pltpu.make_async_copy(source, target, sems.at[i])
        for i, (source, target) in enumerate(zip(sources, held))
    ]
    for load in loads:
        load.start()
    for load in loads:
        load.wait()
    _, channels = query_ref.shape
    for j in range(channels // LANES):
        lanes = pl.ds(j * LANES, LANES)
        mixed = filtered_block(key_ref, tails_ref, taps_ref, 1, lanes) * filtered_block(
            value_ref, tails_ref, taps_ref, 2, lanes
        )
        gate_ref[:, lanes] = filtered_block(query_ref, tails_ref, taps_ref, 0, lanes)
        direct_ref[:, lanes] = gain_ref[:, lanes] * mixed


def gates(query, key_in, value, tails, short_taps, skip_gain):
    shape = jax.ShapeDtypeStruct(query.shape, jnp.float32)
    whole, remote = pl.BlockSpec(memory_space=pltpu.VMEM), pl.BlockSpec(memory_space=pltpu.HBM)
    inputs = [query, key_in, value, short_taps, skip_gain[None, :]]
    return pl.pallas_call(
        gate_kernel,
        out_shape=(shape, shape),
        in_specs=[whole] + [remote] * len(inputs),
        out_specs=(whole, whole),
        scratch_shapes=[
            *(pltpu.VMEM(a.shape, a.dtype) for a in inputs),
            pltpu.SemaphoreType.DMA((len(inputs),)),
        ],
        compiler_params=pltpu.CompilerParams(vmem_limit_bytes=16 * 2**20),
        cost_estimate=pl.CostEstimate(
            flops=20 * query.size, bytes_accessed=14 * query.size, transcendentals=0
        ),
    )(tails, *(pltpu.with_memory_space_constraint(a, pltpu.HBM) for a in inputs))


def column_copies(weight_ref, held, sems, first):
    chunks, _, width = held.shape
    return [
        pltpu.make_async_copy(
            weight_ref.at[:, pl.ds(pl.multiple_of(first + i * width, LANES), width)],
            held.at[i],
            sems.at[i],
        )
        for i in range(chunks)
    ]


def multiply(gated_ref, share_ref, held, copies):
    width = held.shape[2]
    for i, copy in enumerate(copies):
        copy.wait()
        share_ref[:, pl.ds(i * width, width)] = jnp.dot(
            gated_ref[...], held[i], preferred_element_type=jnp.float32
        ).astype(share_ref.dtype)


def gated_kernel(conv_ref, gate_ref, direct_ref, weight_ref, gated_ref, share_ref, held, sems):
    devices, _, block = conv_ref.shape
    columns = weight_ref.shape[1] // 2
    copies = column_copies(weight_ref, held, sems, (1 - lax.axis_index("tp")) * columns)
    for copy in copies:
        copy.start()
    for j in range(devices):
        lanes = pl.ds(j * block, block)
        gated_ref[:, lanes] = (
            gate_ref[:, lanes] * (conv_ref[j].astype(jnp.float32) + direct_ref[:, lanes])
        ).astype(jnp.bfloat16)
    multiply(gated_ref, share_ref, held, copies)


def share_kernel(far, offset, gated_ref, weight_ref, share_ref, held, sems):
    columns = weight_ref.shape[1] // 2
    rank = lax.axis_index("tp")
    copies = column_copies(weight_ref, held, sems, (1 - rank if far else rank) * columns + offset)
    for copy in copies:
        copy.start()
    multiply(gated_ref, share_ref, held, copies)


def projected(convolved, gate_signal, direct, out_weight):
    tokens, channels = gate_signal.shape
    columns = out_weight.shape[1] // 2
    whole, remote = pl.BlockSpec(memory_space=pltpu.VMEM), pl.BlockSpec(memory_space=pltpu.HBM)
    out_weight = pltpu.with_memory_space_constraint(out_weight, pltpu.HBM)

    def share(kernel, operands, extra, width, step, dtype):
        return pl.pallas_call(
            kernel,
            out_shape=(*extra, jax.ShapeDtypeStruct((tokens, width), dtype)),
            in_specs=[whole] * len(operands) + [remote],
            out_specs=(whole,) * (len(extra) + 1),
            scratch_shapes=[
                pltpu.VMEM((width // step, channels, step), jnp.bfloat16),
                pltpu.SemaphoreType.DMA((width // step,)),
            ],
            compiler_params=pltpu.CompilerParams(vmem_limit_bytes=20 * 2**20),
            cost_estimate=pl.CostEstimate(
                flops=2 * tokens * channels * width, bytes_accessed=2 * channels * width, transcendentals=0
            ),
        )(*operands, out_weight)

    swap = [(0, 1), (1, 0)]
    widths = FAR_CHUNKS if sum(FAR_CHUNKS) == columns else (columns,)
    arrived, offset, gated = [], 0, None
    for width in widths:
        if gated is None:
            gated, far = share(
                gated_kernel,
                (convolved, gate_signal, direct),
                (jax.ShapeDtypeStruct((tokens, channels), jnp.bfloat16),),
                width,
                STEP,
                jnp.bfloat16,
            )
        else:
            kernel = functools.partial(share_kernel, True, offset)
            (far,) = share(kernel, (gated,), (), width, STEP, jnp.bfloat16)
        arrived.append(lax.ppermute(far, "tp", swap))
        offset += width
    kernel = functools.partial(share_kernel, False, 0)
    (near,) = share(kernel, (gated,), (), columns, 2 * STEP, jnp.float32)
    return (near + jnp.concatenate(arrived, axis=1).astype(jnp.float32)).astype(jnp.bfloat16)


def butterfly(parts, sign):
    count = len(parts)
    if count == 1:
        return parts
    even, odd = butterfly(parts[0::2], sign), butterfly(parts[1::2], sign)
    half = count // 2
    low, high = [], []
    for j in range(half):
        real, imag = odd[j]
        if 4 * j == count:
            real, imag = (-imag, real) if sign > 0 else (imag, -real)
        elif j:
            c, s = math.cos(2.0 * math.pi * j / count), sign * math.sin(2.0 * math.pi * j / count)
            if 8 * j == count:
                real, imag = ((real - imag) * c, (real + imag) * c) if sign > 0 else ((real + imag) * c, (imag - real) * c)
            elif 8 * j == 3 * count:
                real, imag = ((real + imag) * c, (imag - real) * c) if sign > 0 else ((real - imag) * c, (real + imag) * c)
            else:
                real, imag = real * c - imag * s, real * s + imag * c
        low.append((even[j][0] + real, even[j][1] + imag))
        high.append((even[j][0] - real, even[j][1] - imag))
    return low + high


def turned(pair, cosine, sine):
    real, imag = pair
    return real * cosine - imag * sine, imag * cosine + real * sine


def scaled(pair, factor):
    return turned(pair, *factor)


def powers_of(root):
    powers = [None, root]
    for v in range(2, RADIX):
        powers.append(turned(powers[v // 2], *powers[v - v // 2]))
    return powers


def transform_kernel(
    taken_ref, taps_ref, forward, cos_ref, sin_ref, inverse, out_ref,
    result_ref, packed, inner, flipped, high_ref, low_ref, done, sems, edges,
):
    devices, tokens, block = done.shape
    half = cos_ref.shape[0]
    lane = [pl.ds(v * block, block) for v in range(RADIX)]
    edge = tokens + 2 * half

    edges[:EDGE] = jnp.zeros((EDGE, block), jnp.float32)
    for q in range(devices):
        edges[pl.ds((q + 1) * EDGE, EDGE)] = taken_ref[q, pl.ds(edge, EDGE), :].astype(jnp.float32)

    def ends(index, own):
        return edges[pl.ds(index + EDGE * own, devices, stride=EDGE), :]

    def first_rows(which):
        taps = taps_ref[which]
        base = 2 * (which - 1)
        now, after = ends(base, 1), ends(base + 1, 1)
        older, newer = ends(base + 4, 0), ends(base + 5, 0)
        return (
            taps[0:1] * now + taps[1:2] * newer + taps[2:3] * older,
            taps[0:1] * after + taps[1:2] * now + taps[2:3] * newer,
        )

    key_rows, value_rows = first_rows(1), first_rows(2)
    first_row, second_row = key_rows[0] * value_rows[0], key_rows[1] * value_rows[1]

    def tokens_of(q, v):
        rows = taken_ref[q, pl.ds(v * ROWS, ROWS), :]
        if v > 1:
            return rows
        top = lax.broadcasted_iota(jnp.int32, rows.shape, 0) == 0
        right = (first_row, second_row)[v][q : q + 1]
        return jnp.where(top, right, rows.astype(jnp.float32)).astype(jnp.bfloat16)

    def spectrum_rows(start, imag):
        return pl.ds(tokens + start // GROUP * 2 * GROUP + start % GROUP + imag * GROUP, ROWS)

    part = half // RADIX
    for q in range(devices):
        for v in range(RADIX):
            packed[pl.ds(q * ROWS, ROWS), lane[v]] = tokens_of(q, v)

    row = lax.broadcasted_iota(jnp.int32, (half, half), 0)
    column = lax.broadcasted_iota(jnp.int32, (half, half), 1)
    flip = jnp.where(row + column == half, 1.0, 0.0).astype(jnp.bfloat16)
    for j in range(RADIX):
        source = 2 * RADIX - 1 - 2 * j
        right = jnp.concatenate(
            [
                jnp.concatenate(
                    [
                        taken_ref[source, pl.ds(tokens + (2 * g + imag) * GROUP, GROUP), :]
                        for g in range(half // GROUP)
                    ],
                    axis=0,
                )
                for imag in range(2)
            ],
            axis=1,
        )
        flipped[j] = jnp.dot(flip, right, preferred_element_type=jnp.float32).astype(jnp.bfloat16)

    wide = 2 * block
    for v in range(0, RADIX, 2):
        lanes = pl.ds(v * block, wide)
        right = packed[:, lanes]
        inner[:, lanes] = jnp.dot(forward[...], right, preferred_element_type=jnp.float32)

    def products(rows, start, parts):
        parts = butterfly(parts, -1)
        result = []
        for j in range(RADIX):
            real = taken_ref[2 * j, spectrum_rows(start, 0), :].astype(jnp.float32)
            imag = taken_ref[2 * j, spectrum_rows(start, 1), :].astype(jnp.float32)
            mirror = flipped[j, rows, :].astype(jnp.float32)
            result.append(scaled(parts[j], (real + mirror[:, :block], imag - mirror[:, block:])))
        return butterfly(result, 1)

    def middle(start, first):
        rows = pl.ds(start, ROWS)
        rows_imag = pl.ds(start + half, ROWS)
        top = lax.broadcasted_iota(jnp.int32, (ROWS, block), 0) == 0
        powers = powers_of((cos_ref[rows, :], sin_ref[rows, :]))
        parts, tops = [], []
        for v in range(RADIX):
            real, imag = inner[rows, lane[v]], -inner[rows_imag, lane[v]]
            if first:
                tops.append(-imag)
                imag = jnp.where(top, 0.0, imag)
            if v:
                cosine, sine = powers[v]
                real, imag = turned((real, imag), cosine, -sine)
            parts.append((real, imag))
        parts = products(rows, start, parts)
        if first:
            angles = [math.pi * v / RADIX for v in range(RADIX)]
            nyquist = [(t * math.cos(a), t * -math.sin(a)) for t, a in zip(tops, angles)]
            nyquist = butterfly(nyquist, -1)
            nyquist = [
                scaled(
                    nyquist[j],
                    (
                        taken_ref[2 * j + 1, spectrum_rows(0, 0), :].astype(jnp.float32),
                        taken_ref[2 * j + 1, spectrum_rows(0, 1), :].astype(jnp.float32),
                    ),
                )
                for j in range(RADIX)
            ]
            nyquist = butterfly(nyquist, 1)
            tops = [n[0] * math.cos(a) - n[1] * math.sin(a) for n, a in zip(nyquist, angles)]
        for v in range(RADIX):
            real, imag = parts[v]
            if v:
                real, imag = turned((real, imag), *powers[v])
            imag = jnp.where(top, tops[v], -imag) if first else -imag
            high_ref[rows, lane[v]], low_ref[rows, lane[v]] = split(real)
            high_ref[rows_imag, lane[v]], low_ref[rows_imag, lane[v]] = split(imag)

    middle(0, True)

    @pl.loop(1, half // ROWS)
    def _(i):
        middle(pl.multiple_of(i * ROWS, ROWS), False)

    for v in range(0, RADIX, 2):
        lanes = pl.ds(v * block, wide)
        right = high_ref[:, lanes]
        result = (
            jnp.dot(inverse[...], right, preferred_element_type=jnp.float32)
            + jnp.dot(inverse[...], low_ref[:, lanes], preferred_element_type=jnp.float32)
        ) * (0.5 / (devices * tokens))
        result_ref[:, lanes] = result.astype(jnp.bfloat16)

    matrix = gather_rows(half, RADIX, invert=True)
    copies = []
    for k in range(0, RADIX, 2):
        slabs = [
            jnp.concatenate([result_ref[pl.ds(p * part, part), lane[v]] for v in range(RADIX)], axis=0)
            for p in (k, k + 1)
        ]
        both = exact_rows(matrix, *slabs)
        for q in range(4):
            done[2 * k + q] = both[(q % 2) * tokens : (q % 2 + 1) * tokens, (q // 2) * block : (q // 2 + 1) * block]
        copies.append(
            pltpu.make_async_copy(
                done.at[pl.ds(2 * k, 4)], out_ref.at[pl.ds(2 * k, 4)], sems.at[k // 2]
            )
        )
        copies[-1].start()
    for copy in copies:
        copy.wait()


def angles_of(shape, rows, columns, order):
    index = lax.broadcasted_iota(jnp.int32, shape, rows) * lax.broadcasted_iota(jnp.int32, shape, columns)
    return (2.0 * math.pi / order) * (index & (order - 1)).astype(jnp.float32)


def tables_kernel(forward, cos_ref, sin_ref, inverse):
    depth = forward.shape[1]
    half, block = cos_ref.shape
    order = 2 * RADIX * half

    def alternating(shape, dim):
        return (1 - 2 * (lax.broadcasted_iota(jnp.int32, shape, dim) & 1)).astype(jnp.float32)

    def first(shape, dim):
        return lax.broadcasted_iota(jnp.int32, shape, dim) == 0

    shape = (half, depth)
    angle = angles_of(shape, 0, 1, 2 * half)
    forward[:half] = jnp.cos(angle).astype(jnp.bfloat16)
    sine = jnp.where(first(shape, 0), alternating(shape, 1), jnp.sin(angle))
    forward[half:] = sine.astype(jnp.bfloat16)
    shape = (depth, half)
    angle = angles_of(shape, 0, 1, 2 * half)
    inverse[:, :half] = jnp.cos(angle).astype(jnp.bfloat16)
    sine = jnp.where(first(shape, 1), alternating(shape, 0), jnp.sin(angle))
    inverse[:, half:] = sine.astype(jnp.bfloat16)

    step = lax.broadcasted_iota(jnp.int32, (half, block), 0).astype(jnp.float32)
    angle = (2.0 * math.pi / order) * step
    cos_ref[...] = jnp.cos(angle)
    sin_ref[...] = jnp.sin(angle)


def local_tables(length, block):
    half, depth = length // RADIX, length // RADIX
    whole = pl.BlockSpec(memory_space=pltpu.VMEM)
    forward = jax.ShapeDtypeStruct((2 * half, depth), jnp.bfloat16)
    inverse = jax.ShapeDtypeStruct((depth, 2 * half), jnp.bfloat16)
    twiddle = jax.ShapeDtypeStruct((half, block), jnp.float32)
    return pl.pallas_call(
        tables_kernel,
        out_shape=(forward, twiddle, twiddle, inverse),
        out_specs=(whole,) * 4,
        compiler_params=pltpu.CompilerParams(vmem_limit_bytes=16 * 2**20),
        cost_estimate=pl.CostEstimate(
            flops=200 * RADIX * half * block, bytes_accessed=8 * RADIX * half * block, transcendentals=0
        ),
    )()


def local_transform(taken, taps, tables, tokens):
    devices, _, block = taken.shape
    length = devices * tokens
    half, depth = length // RADIX, length // RADIX
    flops = 3 * 2 * 2 * half * depth * RADIX * block
    whole, remote = pl.BlockSpec(memory_space=pltpu.VMEM), pl.BlockSpec(memory_space=pltpu.HBM)
    wide = RADIX * block
    return pl.pallas_call(
        transform_kernel,
        out_shape=pltpu.HBM((devices, tokens, block), jnp.bfloat16),
        in_specs=[whole] * 6,
        out_specs=remote,
        scratch_shapes=[
            pltpu.VMEM((depth, wide), jnp.bfloat16),
            pltpu.VMEM((depth, wide), jnp.bfloat16),
            pltpu.VMEM((2 * half, wide), jnp.float32),
            pltpu.VMEM((RADIX, half, 2 * block), jnp.bfloat16),
            pltpu.VMEM((2 * half, wide), jnp.bfloat16),
            pltpu.VMEM((2 * half, wide), jnp.bfloat16),
            pltpu.VMEM((devices, tokens, block), jnp.bfloat16),
            pltpu.SemaphoreType.DMA((RADIX // 2,)),
            pltpu.VMEM(((devices + 1) * EDGE, block), jnp.float32),
        ],
        compiler_params=pltpu.CompilerParams(vmem_limit_bytes=20 * 2**20),
        cost_estimate=pl.CostEstimate(flops=flops, bytes_accessed=taken.size * 2, transcendentals=0),
    )(taken, taps, *tables)


def sum_shares(share, axis):
    count = lax.axis_size(axis)
    rank = lax.axis_index(axis)
    columns = share.shape[1] // count
    total = lax.dynamic_slice_in_dim(share, rank * columns, columns, axis=1)
    for step in range(1, count):
        piece = lax.dynamic_slice_in_dim(share, (rank + step) % count * columns, columns, axis=1)
        pairs = [(i, (i + step) % count) for i in range(count)]
        total = total + lax.ppermute(piece.astype(jnp.bfloat16), axis, pairs).astype(jnp.float32)
    return total


def fused_shards(query, key_in, value, short_taps, skip_gain, filter_spectrum, out_weight):
    devices = lax.axis_size("ctx")
    tokens, channels = query.shape
    block = channels // devices
    sent = prepared(key_in, value, short_taps, filter_spectrum, devices)
    taken = lax.all_to_all(sent, "ctx", split_axis=0, concat_axis=0, tiled=True)
    tails = own_tails(query, key_in, value)
    tails = shifted_in(tails, "ctx")
    gate_signal, direct = gates(query, key_in, value, tails, short_taps, skip_gain)
    own_taps = lax.dynamic_slice_in_dim(short_taps, lax.axis_index("ctx") * block, block, axis=2)
    tables = local_tables(tokens * devices, block)
    convolved = local_transform(taken, own_taps, tables, tokens)
    convolved = lax.all_to_all(convolved, "ctx", split_axis=0, concat_axis=0, tiled=True)
    return projected(convolved, gate_signal, direct, out_weight)


def shards(query, key_in, value, short_taps, skip_gain, filter_spectrum, out_weight):
    devices = lax.axis_size("ctx")
    tokens, channels = query.shape
    length, block = tokens * devices, channels // devices
    if block == LANES and devices == 2 * RADIX and tokens == ROWS * RADIX and lax.axis_size("tp") == 2:
        return fused_shards(query, key_in, value, short_taps, skip_gain, filter_spectrum, out_weight)
    tails = shifted_in(jnp.concatenate([query[-2:], key_in[-2:], value[-2:]], axis=0), "ctx")
    gate_signal = causal_filter(query, tails[0:2], short_taps[0])
    mixed_in = causal_filter(key_in, tails[2:4], short_taps[1]) * causal_filter(
        value, tails[4:6], short_taps[2]
    )
    own_signal = mixed_in.astype(jnp.bfloat16).reshape(tokens, devices, block).transpose(1, 0, 2)
    own_spectrum = (
        filter_spectrum.astype(jnp.bfloat16)
        .reshape(tokens, 2, 2, devices, block)
        .transpose(3, 2, 0, 1, 4)
        .reshape(devices, 4 * tokens, block)
    )
    sent = jnp.concatenate([own_signal, own_spectrum], axis=1)
    taken = lax.all_to_all(sent, "ctx", split_axis=0, concat_axis=0, tiled=True)
    signal = taken[:, :tokens].reshape(length, block)
    spectrum_real = taken[:, tokens : 3 * tokens].reshape(2 * length, block)
    spectrum_imag = taken[:, 3 * tokens :].reshape(2 * length, block)
    convolved = long_filter(signal, spectrum_real, spectrum_imag).astype(jnp.bfloat16)
    convolved = lax.all_to_all(
        convolved.reshape(devices, tokens, block), "ctx", split_axis=0, concat_axis=0, tiled=True
    )
    convolved = convolved.transpose(1, 0, 2).reshape(tokens, channels).astype(jnp.float32)
    gated = (gate_signal * (convolved + skip_gain * mixed_in)).astype(jnp.bfloat16)
    share = jnp.dot(gated, out_weight, preferred_element_type=jnp.float32)
    return sum_shares(share, "tp").astype(jnp.bfloat16)


def solution(mesh):
    return jax.shard_map(
        shards,
        mesh=mesh,
        in_specs=(
            P("ctx", "tp"),
            P("ctx", "tp"),
            P("ctx", "tp"),
            P(None, None, "tp"),
            P("tp"),
            P("ctx", None, None, "tp"),
            P("tp", None),
        ),
        out_specs=P("ctx", "tp"),
        check_vma=False,
    )
```
